32 devices in a mesh: group: 2 (over x), ctx: 8 (over z, y), head: 2 (over core).
Axes of the slice: x: 2, y: 2, z: 4, core: 2. Of those that a mesh axis runs over, the one named last changes fastest.
Arguments:
- queries: bfloat16 [12288, 4096], P(('group', 'ctx'), 'head'), parts along dimension 0, may hold values from -160 to 160
- keys: bfloat16 [12288, 1024], P(('group', 'ctx'), 'head'), parts along dimension 0, may hold values from -6 to 6
- values: bfloat16 [12288, 1024], P(('group', 'ctx'), 'head'), parts along dimension 0, may hold values from -6 to 6
- vertical: int32 [16, 16], P(('group', 'head')), parts along dimension 0, may hold values from 0 to 95, as said below
- vert_count: int32 [16], P(('group', 'head')), parts along dimension 0, may hold values from 8 to 16, as said below
- slash: int32 [16, 4], P(('group', 'head')), parts along dimension 0, may hold values from 0 to 5, as said below
- slash_count: int32 [16], P(('group', 'head')), parts along dimension 0, may hold values from 1 to 4, as said below
Outputs:
- attended: bfloat16 [12288, 4096], P(('group', 'ctx'), 'head'), parts along dimension 0
The draws below stay inside these ranges and needn't reach their ends.
There are 2 independent parts, one for each index of `group`. The reference program is written for one: setup_inputs(seed, part) draws one part's arguments, and reference() takes and returns one part's arrays. A program takes and returns all parts, laid end to end along the dimension named above; each array names one. Nothing has to cross between parts.
Inputs may be any that keep to these rules, and one draw needn't show every extreme that they name: `vertical`: entries past a head's count are ignored. A head's 16 entries are distinct; at most 2 of them lie in one span of 12 blocks held by one index of ctx, and a head's first two entries lie in one such span. `vert_count`: some head has all 16 entries live. `slash`: entries past a head's count are ignored. A head's entries are distinct and its first is 0; some head with all 4 entries live has the offset 6 - 1. `slash_count`: some head has all 4 entries live.
All inputs are finite; a program needn't handle non-finite values.
Results may differ from the reference program's by a relative error of at most 0.0036.
Values may be sent and summed in bfloat16 or wider, within the bound.
A program may use at most 128 MiB of HBM per device.

```python
import math
import jax
import jax.numpy as jnp
from jax import lax

HQ = 32
KVH = 8
HD = 128
BLK = 64
NV = 16
NS = 4
MAXOFF = 6
VCAP = 2
TOK_DEV = 768
SEQ = 6144
BLK_DEV = 12
NB = 96


def shared_fields(key):
    base_k = jnp.clip(jax.random.normal(jax.random.fold_in(key, 101), (SEQ, KVH * HD), jnp.float32), -6.0, 6.0)
    base_q = jnp.clip(2.0 * jax.random.normal(jax.random.fold_in(key, 102), (SEQ, HQ * HD), jnp.float32), -12.0, 12.0)
    return (base_k, base_q)


def draw_queries(key, part):
    return shared_fields(key)[1].astype(jnp.bfloat16)


def draw_keys(key, part):
    return shared_fields(key)[0].astype(jnp.bfloat16)


def draw_vertical(key, part):
    spans = NB // BLK_DEV

    def one_head(head_key):
        order = jax.random.permutation(jax.random.fold_in(head_key, 1), spans * VCAP).astype(jnp.int32)
        partner = order[0] - order[0] % VCAP + (order[0] % VCAP + 1) % VCAP
        where_partner = jnp.argmax(order == partner)
        second = order[1]
        order = order.at[where_partner].set(second).at[1].set(partner)
        order = order[:NV]
        offsets = jax.random.randint(jax.random.fold_in(head_key, 2), (spans,), 0, BLK_DEV)
        span_of = order // VCAP
        within = order % VCAP
        inner = (offsets[span_of] + within) % BLK_DEV
        return (span_of * BLK_DEV + inner).astype(jnp.int32)
    head_keys = jax.random.split(jax.random.fold_in(key, 201), KVH)
    return jax.vmap(one_head)(head_keys)


def draw_vert_count(key, part):
    counts = jax.random.randint(jax.random.fold_in(key, 211), (KVH,), NV // 2, NV + 1)
    fullest = jax.random.randint(jax.random.fold_in(key, 212), (), 0, KVH)
    return jnp.where(jnp.arange(KVH) == fullest, NV, counts).astype(jnp.int32)


def slash_head_choice(key):
    return jax.random.randint(jax.random.fold_in(key, 301), (), 0, KVH)


def draw_slash(key, part):
    chosen = slash_head_choice(key)

    def one_head(head_key, head_id):
        common = jax.random.permutation(jax.random.fold_in(head_key, 1), MAXOFF - 1)[:NS - 1] + 1
        forced = jnp.concatenate([jax.random.permutation(jax.random.fold_in(head_key, 2), MAXOFF - 2)[:NS - 2] + 1, jnp.full((1,), MAXOFF - 1)])
        rest = jnp.where(head_id == chosen, forced, common)
        return jnp.concatenate([jnp.zeros((1,), jnp.int32), rest.astype(jnp.int32)])
    head_keys = jax.random.split(jax.random.fold_in(key, 302), KVH)
    return jax.vmap(one_head)(head_keys, jnp.arange(KVH)).astype(jnp.int32)


def draw_slash_count(key, part):
    chosen = slash_head_choice(key)
    counts = jax.random.randint(jax.random.fold_in(key, 311), (KVH,), 1, NS + 1)
    return jnp.where(jnp.arange(KVH) == chosen, NS, counts).astype(jnp.int32)


def steps_of(own_key, shape, pieces, low, top_value):
    loudness = 1.0
    for dim, shards_of in pieces:
        steps = jax.random.uniform(jax.random.fold_in(jax.random.fold_in(own_key, 6), dim), (shards_of,), jnp.float32, low / len(pieces), top_value / len(pieces))
        loudness = loudness * jnp.repeat(jnp.exp(steps), shape[dim] // shards_of).reshape((-1,) + (1,) * (len(shape) - 1 - dim))
    return loudness


def scatter_about(stream_key, shape, spread, bound, shards=(), held_as=jnp.bfloat16):
    array = spread * jax.random.normal(stream_key, shape, jnp.float32)
    if shards:
        array = array * steps_of(stream_key, shape, shards, -0.22, 0.18)
    return jnp.clip(array, -bound, bound).astype(held_as)


def setup_inputs(seed: int = 0, part: int = 0) -> dict:
    arg_keys = jax.random.split(jax.random.key(seed), 8)
    part_keys = jax.random.split(jax.random.fold_in(arg_keys[7], part), 8)
    queries = draw_queries(jax.random.fold_in(jax.random.fold_in(arg_keys[7], part), 71), part)
    keys = draw_keys(jax.random.fold_in(jax.random.fold_in(arg_keys[7], part), 71), part)
    values = scatter_about(part_keys[2], (SEQ, KVH * HD), 1.0, 6.0, ((0, 8), (1, 2)))
    vertical = draw_vertical(jax.random.fold_in(jax.random.fold_in(arg_keys[7], part), 71), part)
    vert_count = draw_vert_count(jax.random.fold_in(jax.random.fold_in(arg_keys[7], part), 71), part)
    slash = draw_slash(jax.random.fold_in(jax.random.fold_in(arg_keys[7], part), 71), part)
    slash_count = draw_slash_count(jax.random.fold_in(jax.random.fold_in(arg_keys[7], part), 71), part)
    return {"queries": queries, "keys": keys, "values": values, "vertical": vertical, "vert_count": vert_count, "slash": slash, "slash_count": slash_count}


NEG = -1e+30

def attend_head(q_head, vert_kv, vert_blocks, vert_live, slash_kv, slash_src, slash_ok, qpos_rows, scale):
    tok_rows, per_group, width = q_head.shape
    blocks_dev, slash_n, blk, _ = slash_kv.shape
    vert_n = vert_kv.shape[0]
    vert_keys = vert_kv[:, :, :width].reshape(vert_n * blk, width).astype(jnp.float32)
    vert_vals = vert_kv[:, :, width:].reshape(vert_n * blk, width).astype(jnp.float32)
    vert_scores = jnp.einsum('tgd,kd->gtk', q_head.astype(jnp.float32), vert_keys) * scale
    key_pos = (vert_blocks[:, None] * blk + jnp.arange(blk)[None, :]).reshape(-1)
    live_cols = jnp.repeat(vert_live, blk)
    vert_mask = live_cols[None, :] & (key_pos[None, :] <= qpos_rows[:, None])
    vert_scores = jnp.where(vert_mask[None], vert_scores, NEG)
    q_blocks = q_head.reshape(blocks_dev, blk, per_group, width).astype(jnp.float32)
    slash_keys = slash_kv[..., :width].reshape(blocks_dev, slash_n * blk, width).astype(jnp.float32)
    slash_vals = slash_kv[..., width:].reshape(blocks_dev, slash_n * blk, width).astype(jnp.float32)
    slash_scores = jnp.einsum('lbgd,lkd->glbk', q_blocks, slash_keys) * scale
    slash_pos = (slash_src[:, :, None] * blk + jnp.arange(blk)[None, None, :]).reshape(blocks_dev, slash_n * blk)
    slash_cols = jnp.repeat(slash_ok, blk, axis=1)
    qpos_blocks = qpos_rows.reshape(blocks_dev, blk)
    slash_mask = slash_cols[:, None, :] & (slash_pos[:, None, :] <= qpos_blocks[:, :, None])
    slash_scores = jnp.where(slash_mask[None], slash_scores, NEG)
    row_top = jnp.maximum(lax.optimization_barrier(jnp.max(vert_scores, axis=2)).reshape(per_group, blocks_dev, blk), lax.optimization_barrier(jnp.max(slash_scores, axis=3)))
    vert_prob = jnp.exp(vert_scores - row_top.reshape(per_group, tok_rows)[:, :, None])
    slash_prob = jnp.exp(slash_scores - row_top[..., None])
    total = lax.optimization_barrier(jnp.sum(vert_prob, axis=2)).reshape(per_group, blocks_dev, blk) + lax.optimization_barrier(jnp.sum(slash_prob, axis=3))
    vert_weight = lax.optimization_barrier(vert_prob.astype(jnp.bfloat16)).astype(jnp.float32)
    slash_weight = lax.optimization_barrier(slash_prob.astype(jnp.bfloat16)).astype(jnp.float32)
    vert_out = jnp.einsum('gtk,kd->gtd', vert_weight, vert_vals).reshape(per_group, blocks_dev, blk, width)
    slash_out = jnp.einsum('glbk,lkd->glbd', slash_weight, slash_vals)
    mixed = ((vert_out + slash_out) / total[..., None]).astype(jnp.bfloat16)
    return mixed.transpose(1, 2, 0, 3).reshape(tok_rows, per_group * width)

def reference(queries, keys, values, vertical, vert_count, slash, slash_count):
    seq_len = queries.shape[0]
    block_count = seq_len // BLK
    span_blocks = TOK_DEV // BLK
    per_group = HQ // KVH
    scale = 1.0 / math.sqrt(HD)
    key_heads = keys.reshape(block_count, BLK, KVH, HD).transpose(2, 0, 1, 3)
    val_heads = values.reshape(block_count, BLK, KVH, HD).transpose(2, 0, 1, 3)
    table_all = jnp.concatenate([key_heads, val_heads], axis=3)
    q_heads = queries.reshape(seq_len, KVH, per_group, HD).transpose(1, 0, 2, 3)

    def one_head(args):
        q_head, table, vert_blocks, vert_n, slash_offs, slash_n = args
        vert_live = jnp.arange(NV) < vert_n
        vert_kv = table[vert_blocks]
        slash_live = jnp.arange(NS) < slash_n

        def one_span(span_id):
            start = (span_id * TOK_DEV).astype(jnp.int32)
            q_span = lax.dynamic_slice_in_dim(q_head, start, TOK_DEV, 0)
            block_ids = span_id * span_blocks + jnp.arange(span_blocks)
            slash_src = block_ids[:, None] - slash_offs[None, :]
            is_vertical = jnp.any(vert_live[None, None, :] & (vert_blocks[None, None, :] == slash_src[:, :, None]), axis=2)
            slash_ok = slash_live[None, :] & (slash_src >= 0) & jnp.logical_not(is_vertical)
            slash_kv = table[jnp.clip(slash_src, 0, block_count - 1)]
            qpos_rows = span_id * TOK_DEV + jnp.arange(TOK_DEV)
            return attend_head(q_span, vert_kv, vert_blocks, vert_live, slash_kv, slash_src, slash_ok, qpos_rows, scale)
        spans = lax.map(one_span, jnp.arange(seq_len // TOK_DEV))
        return spans.reshape(seq_len, per_group * HD)
    heads = lax.map(one_head, (q_heads, table_all, vertical, vert_count, slash, slash_count))
    return heads.transpose(1, 0, 2).reshape(seq_len, HQ * HD)
```

```python
from functools import partial
import math

import jax
import jax.numpy as jnp
from jax import lax
from jax.experimental import pallas as pl
from jax.experimental.pallas import tpu as pltpu
from jax.sharding import PartitionSpec as P

HD = 128
BLK = 64
NV = 16
NS = 4
VCAP = 2
HALO = 5
CHUNK = 4
NEG = -1e30


def pack_kernel(vert_ref, count_ref, keys_ref, vals_ref, out_ref, *, heads, span):
    lo = lax.axis_index("ctx") * span
    for h in range(heads):
        count = count_ref[h]
        first = jnp.int32(0)
        second = jnp.int32(0)
        seen = jnp.int32(0)
        for s in range(NV):
            at = vert_ref[h, s] - lo
            own = (s < count) & (at >= 0) & (at < span)
            first = jnp.where(own & (seen == 0), at, first)
            second = jnp.where(own & (seen == 1), at, second)
            seen = seen + own.astype(jnp.int32)
        cols = slice(h * HD, (h + 1) * HD)
        for r, blk in enumerate((first, second)):
            rows = pl.ds(pl.multiple_of(blk * BLK, BLK), BLK)
            out_ref[h, r * BLK : (r + 1) * BLK, :HD] = keys_ref[rows, cols]
            out_ref[h, r * BLK : (r + 1) * BLK, HD:] = vals_ref[rows, cols]


def attend_kernel(
    vert_ref, vcount_ref, slash_ref, scount_ref,
    q_ref, k_ref, v_ref, lk_ref, lv_ref, all_ref, out_ref,
    kbuf, vbuf, kext, vext, used, near, own,
    *, span, group, spans,
):
    h = pl.program_id(0)
    lo = lax.axis_index("ctx") * span
    coef = math.log2(math.e) / math.sqrt(HD)

    @pl.when(h == 0)
    def _():
        kbuf[...] = jnp.zeros_like(kbuf)
        vbuf[:, :HD] = jnp.zeros((vbuf.shape[0], HD), jnp.bfloat16)
        vbuf[:, HD:] = jnp.ones((vbuf.shape[0], HD), jnp.bfloat16)

    halo = HALO * BLK
    kext[:halo, :] = lk_ref[...]
    vext[:halo, :] = lv_ref[...]
    kext[halo:, :] = k_ref[...]
    vext[halo:, :] = v_ref[...]
    for i in range(spans):
        used[i] = 0
    for i in range(HALO + span):
        near[i] = 0

    def take(n, at):
        to = pl.ds(pl.multiple_of(n * BLK, BLK), BLK)
        rows = pl.ds(pl.multiple_of(at * BLK, BLK), BLK)
        kbuf[to, :] = kext[rows, :]
        vbuf[to, :HD] = vext[rows, :]

    count = vcount_ref[h]

    def entry(s, state):
        n, mine = state
        blk = vert_ref[h, s]
        owner = blk // span
        rank = used[owner]
        used[owner] = rank + 1
        clean = blk < lo
        in_own = (blk >= lo) & (blk < lo + span)

        @pl.when(clean)
        def _():
            to = pl.ds(pl.multiple_of(n * BLK, BLK), BLK)
            rows = pl.ds(pl.multiple_of(rank * BLK, BLK), BLK)
            kbuf[to, :] = all_ref[owner, 0, rows, :HD]
            vbuf[to, :HD] = all_ref[owner, 0, rows, HD:]

        @pl.when(in_own)
        def _():
            own[mine] = blk - lo

        at = blk - lo + HALO

        @pl.when((at >= 0) & (at < HALO + span))
        def _():
            near[at] = 1

        return n + clean.astype(jnp.int32), mine + in_own.astype(jnp.int32)

    shared, mine = lax.fori_loop(0, count, entry, (jnp.int32(1), jnp.int32(0)))
    slashes = scount_ref[h]

    def body(chunks, l, n):
        width = chunks * CHUNK * BLK
        rows = pl.ds(pl.multiple_of(l * BLK, BLK), BLK)
        q = jnp.concatenate(
            [q_ref[rows, g * HD : (g + 1) * HD] for g in range(group)], axis=0
        )
        s = lax.dot_general(
            q, kbuf[:width, :], (((1,), (1,)), ((), ())), preferred_element_type=jnp.float32
        )
        tall = group * BLK
        tri_row = lax.broadcasted_iota(jnp.int32, (tall, 2 * BLK), 0) % BLK
        tri_col = lax.broadcasted_iota(jnp.int32, (tall, 2 * BLK), 1)
        head = jnp.where((tri_col <= tri_row) | (tri_col >= BLK), s[:, : 2 * BLK], NEG)
        tail_at = width - (CHUNK - 1) * BLK
        tail_at = tail_at // (2 * BLK) * (2 * BLK)
        parts = [head]
        live = n * BLK
        for c in range(2 * BLK, width, 2 * BLK):
            part = s[:, c : c + 2 * BLK]
            parts.append(part)
        for i in range(len(parts)):
            c = i * 2 * BLK
            if c >= tail_at:
                col = lax.broadcasted_iota(jnp.int32, (tall, 2 * BLK), 1) + c
                parts[i] = jnp.where(col < live, parts[i], NEG)
        s = jnp.concatenate(parts, axis=1)
        top = jnp.max(s, axis=1, keepdims=True)
        p = jnp.exp2((s - top) * coef).astype(jnp.bfloat16)
        o = jnp.dot(p, vbuf[:width, :], preferred_element_type=jnp.float32)
        o = (o[:, :HD] / o[:, HD:]).astype(jnp.bfloat16)
        for g in range(group):
            out_ref[rows, g * HD : (g + 1) * HD] = o[g * BLK : (g + 1) * BLK, :]

    def row_block(l, carry):
        take(0, l + HALO)
        n = shared
        for i in range(VCAP):
            use = (i < mine) & (own[i] < l)

            @pl.when(use)
            def _():
                take(n, own[i] + HALO)

            n = n + use.astype(jnp.int32)
        for j in range(1, NS):
            at = l + HALO - slash_ref[h, j]
            use = (j < slashes) & (at + lo >= HALO)
            use = use & (near[at] == 0)

            @pl.when(use)
            def _():
                take(n, at)

            n = n + use.astype(jnp.int32)
        chunks = (n + CHUNK - 1) // CHUNK
        for c in range(1, (NV + NS) // CHUNK + 1):

            @pl.when(chunks == c)
            def _():
                body(c, l, n)

        return carry

    lax.fori_loop(0, span, row_block, 0)


def local(spans, queries, keys, values, vertical, vert_count, slash, slash_count):
    tok_rows = queries.shape[0]
    heads = keys.shape[1] // HD
    group = queries.shape[1] // keys.shape[1]
    span = tok_rows // BLK
    halo = HALO * BLK
    smem = pl.BlockSpec(memory_space=pltpu.SMEM)
    tail = jnp.concatenate([keys[tok_rows - halo :], values[tok_rows - halo :]], axis=1)
    left = lax.ppermute(tail, "ctx", [(i, i + 1) for i in range(spans - 1)])
    packed = pl.pallas_call(
        partial(pack_kernel, heads=heads, span=span),
        out_shape=jax.ShapeDtypeStruct((heads, VCAP * BLK, 2 * HD), jnp.bfloat16),
        in_specs=[smem, smem, pl.BlockSpec(), pl.BlockSpec()],
        out_specs=pl.BlockSpec(),
        name="pack",
    )(vertical, vert_count, keys, values)
    everyone = lax.all_gather(packed, "ctx", axis=0)
    cap = (NV + NS) * BLK
    return pl.pallas_call(
        partial(attend_kernel, span=span, group=group, spans=spans),
        grid=(heads,),
        out_shape=jax.ShapeDtypeStruct(queries.shape, jnp.bfloat16),
        in_specs=[
            smem, smem, smem, smem,
            pl.BlockSpec((tok_rows, group * HD), lambda h: (0, h)),
            pl.BlockSpec((tok_rows, HD), lambda h: (0, h)),
            pl.BlockSpec((tok_rows, HD), lambda h: (0, h)),
            pl.BlockSpec((halo, HD), lambda h: (0, h)),
            pl.BlockSpec((halo, HD), lambda h: (0, h + heads)),
            pl.BlockSpec((spans, 1, VCAP * BLK, 2 * HD), lambda h: (0, h, 0, 0)),
        ],
        out_specs=pl.BlockSpec((tok_rows, group * HD), lambda h: (0, h)),
        scratch_shapes=[
            pltpu.VMEM((cap, HD), jnp.bfloat16),
            pltpu.VMEM((cap, 2 * HD), jnp.bfloat16),
            pltpu.VMEM((halo + tok_rows, HD), jnp.bfloat16),
            pltpu.VMEM((halo + tok_rows, HD), jnp.bfloat16),
            pltpu.SMEM((spans,), jnp.int32),
            pltpu.SMEM((HALO + span,), jnp.int32),
            pltpu.SMEM((VCAP,), jnp.int32),
        ],
        compiler_params=pltpu.CompilerParams(vmem_limit_bytes=40 * 2**20),
        name="attend",
    )(vertical, vert_count, slash, slash_count, queries, keys, values, left, left, everyone)


def solution(mesh):
    placed = (
        P(("group", "ctx"), "head"),
        P(("group", "ctx"), "head"),
        P(("group", "ctx"), "head"),
        P(("group", "head"), None),
        P(("group", "head")),
        P(("group", "head"), None),
        P(("group", "head")),
    )
    return jax.shard_map(
        partial(local, mesh.shape["ctx"]),
        mesh=mesh, in_specs=placed, out_specs=P(("group", "ctx"), "head"), check_vma=False,
    )
```

```python
from functools import partial
import math

import jax
import jax.numpy as jnp
from jax import lax
from jax.experimental import pallas as pl
from jax.experimental.pallas import tpu as pltpu
from jax.sharding import PartitionSpec as P

HD = 128
BLK = 64
NV = 16
NS = 4
VCAP = 2
HALO = 5
CHUNK = 4
NEG = -1e30
UNROLL = 2
TOGETHER = 2


def pack_kernel(vert_ref, count_ref, keys_ref, vals_ref, *out_refs, heads, span):
    lo = lax.axis_index("ctx") * span
    for h in range(heads):
        count = count_ref[h]
        first = jnp.int32(0)
        second = jnp.int32(0)
        seen = jnp.int32(0)
        for s in range(NV):
            at = vert_ref[h, s] - lo
            own = (s < count) & (at >= 0) & (at < span)
            first = jnp.where(own & (seen == 0), at, first)
            second = jnp.where(own & (seen == 1), at, second)
            seen = seen + own.astype(jnp.int32)
        cols = slice(h * HD, (h + 1) * HD)
        for r, blk in enumerate((first, second)):
            rows = pl.ds(pl.multiple_of(blk * BLK, BLK), BLK)
            to = slice(r * BLK, (r + 1) * BLK)
            out_ref = out_refs[h // TOGETHER]
            out_ref[h % TOGETHER, to, :HD] = keys_ref[rows, cols]
            out_ref[h % TOGETHER, to, HD:] = vals_ref[rows, cols]


def attend_kernel(
    vert_ref, vcount_ref, slash_ref, scount_ref,
    q_ref, k_ref, v_ref, lk_ref, lv_ref, all_ref, *rest,
    span, group, spans, first_head,
):
    out_ref, kbuf, vbuf, kext, vext, used, near, own = rest[-8:]
    h = pl.program_id(0) + first_head
    lo = lax.axis_index("ctx") * span
    coef = math.log2(math.e) / math.sqrt(HD)

    @pl.when(pl.program_id(0) == 0)
    def _():
        kbuf[...] = jnp.zeros_like(kbuf)
        vbuf[:, :, :HD] = jnp.zeros(vbuf.shape[:2] + (HD,), jnp.bfloat16)
        vbuf[:, :, HD:] = jnp.ones(vbuf.shape[:2] + (HD,), jnp.bfloat16)

    halo = HALO * BLK
    kext[:halo, :] = lk_ref[...]
    vext[:halo, :] = lv_ref[...]
    kext[halo:, :] = k_ref[...]
    vext[halo:, :] = v_ref[...]
    for i in range(spans):
        used[i] = 0
    for i in range(HALO + span):
        near[i] = 0

    def take(u, n, at):
        to = pl.ds(pl.multiple_of(n * BLK, BLK), BLK)
        rows = pl.ds(pl.multiple_of(at * BLK, BLK), BLK)
        kbuf[u, to, :] = kext[rows, :]
        vbuf[u, to, :HD] = vext[rows, :]

    count = vcount_ref[h]

    def entry(s, state):
        n, mine = state
        blk = vert_ref[h, s]
        owner = blk // span
        rank = used[owner]
        used[owner] = rank + 1
        clean = blk < lo
        in_own = (blk >= lo) & (blk < lo + span)

        @pl.when(clean)
        def _():
            to = pl.ds(pl.multiple_of(n * BLK, BLK), BLK)
            rows = pl.ds(pl.multiple_of(rank * BLK, BLK), BLK)
            k_blk = all_ref[owner, 0, rows, :HD]
            v_blk = all_ref[owner, 0, rows, HD:]
            for u in range(UNROLL):
                kbuf[u, to, :] = k_blk
                vbuf[u, to, :HD] = v_blk

        @pl.when(in_own)
        def _():
            own[mine] = blk - lo

        at = blk - lo + HALO

        @pl.when((at >= 0) & (at < HALO + span))
        def _():
            near[at] = 1

        return n + clean.astype(jnp.int32), mine + in_own.astype(jnp.int32)

    shared, mine = lax.fori_loop(0, count, entry, (jnp.int32(1), jnp.int32(0)))
    slashes = scount_ref[h]
    tall = group * BLK
    pair = 2 * BLK

    def scores(u, chunks, l, n):
        width = chunks * CHUNK * BLK
        rows = pl.ds(pl.multiple_of(l * BLK, BLK), BLK)
        q = jnp.concatenate(
            [q_ref[rows, g * HD : (g + 1) * HD] for g in range(group)], axis=0
        )
        s = lax.dot_general(
            q, kbuf[u, :width, :], (((1,), (1,)), ((), ())), preferred_element_type=jnp.float32
        )
        row = lax.broadcasted_iota(jnp.int32, (tall, pair), 0) % BLK
        col = lax.broadcasted_iota(jnp.int32, (tall, pair), 1)
        parts = []
        for c in range(0, width, pair):
            part = s[:, c : c + pair]
            if c >= width - 2 * CHUNK * BLK:
                part = jnp.where(col < n * BLK - c, part, NEG)
            if c == 0:
                part = jnp.where((col <= row) | (col >= BLK), part, NEG)
            parts.append(part)
        return parts

    def body(chunks, ls, ns):
        width = chunks * CHUNK * BLK
        all_parts = [scores(u, chunks, l, n) for u, (l, n) in enumerate(zip(ls, ns))]
        probs = []
        for parts in all_parts:
            top = parts[0]
            for part in parts[1:]:
                top = jnp.maximum(top, part)
            top = jnp.max(top, axis=1, keepdims=True)
            probs.append(
                jnp.concatenate(
                    [jnp.exp2((part - top) * coef).astype(jnp.bfloat16) for part in parts], axis=1
                )
            )
        for u, (l, p) in enumerate(zip(ls, probs)):
            rows = pl.ds(pl.multiple_of(l * BLK, BLK), BLK)
            o = jnp.dot(p, vbuf[u, :width, :], preferred_element_type=jnp.float32)
            o = (o[:, :HD] / o[:, HD:]).astype(jnp.bfloat16)
            for g in range(group):
                out_ref[rows, g * HD : (g + 1) * HD] = o[g * BLK : (g + 1) * BLK, :]

    def fill(u, l):
        take(u, 0, l + HALO)
        n = shared
        for i in range(VCAP):
            use = (i < mine) & (own[i] < l)

            @pl.when(use)
            def _():
                take(u, n, own[i] + HALO)

            n = n + use.astype(jnp.int32)
        for j in range(1, NS):
            at = l + HALO - slash_ref[h, j]
            use = (j < slashes) & (at + lo >= HALO)
            use = use & (near[at] == 0)

            @pl.when(use)
            def _():
                take(u, n, at)

            n = n + use.astype(jnp.int32)
        return n

    def row_blocks(i, carry):
        ls = [i * UNROLL + u for u in range(UNROLL)]
        ns = [fill(u, l) for u, l in enumerate(ls)]
        most = ns[0]
        for n in ns[1:]:
            most = jnp.maximum(most, n)
        chunks = (most + CHUNK - 1) // CHUNK
        for c in range(1, (NV + NS) // CHUNK + 1):

            @pl.when(chunks == c)
            def _():
                body(c, ls, ns)

        return carry

    lax.fori_loop(0, span // UNROLL, row_blocks, 0)


def attend(tables, queries, keys, values, left, everyone, out, first_head, heads, spans):
    tok_rows, all_cols = queries.shape
    kv_heads = keys.shape[1] // HD
    wide = all_cols // kv_heads
    span = tok_rows // BLK
    halo = HALO * BLK
    cap = (NV + NS) * BLK
    smem = pl.BlockSpec(memory_space=pltpu.SMEM)
    operands = [*tables, queries, keys, values, left, left, everyone]
    in_specs = [
        smem, smem, smem, smem,
        pl.BlockSpec((tok_rows, wide), lambda h: (0, h + first_head)),
        pl.BlockSpec((tok_rows, HD), lambda h: (0, h + first_head)),
        pl.BlockSpec((tok_rows, HD), lambda h: (0, h + first_head)),
        pl.BlockSpec((halo, HD), lambda h: (0, h + first_head)),
        pl.BlockSpec((halo, HD), lambda h: (0, h + first_head + kv_heads)),
        pl.BlockSpec((spans, 1, VCAP * BLK, 2 * HD), lambda h: (0, h, 0, 0)),
    ]
    aliases = {}
    if out is not None:
        aliases = {len(operands): 0}
        operands.append(out)
        in_specs.append(pl.BlockSpec(memory_space=pl.ANY))
    flops = 2 * 2 * tok_rows * wide * cap * heads
    return pl.pallas_call(
        partial(
            attend_kernel, span=span, group=wide // HD, spans=spans, first_head=first_head
        ),
        grid=(heads,),
        out_shape=jax.ShapeDtypeStruct(queries.shape, jnp.bfloat16),
        in_specs=in_specs,
        out_specs=pl.BlockSpec((tok_rows, wide), lambda h: (0, h + first_head)),
        scratch_shapes=[
            pltpu.VMEM((UNROLL, cap, HD), jnp.bfloat16),
            pltpu.VMEM((UNROLL, cap, 2 * HD), jnp.bfloat16),
            pltpu.VMEM((halo + tok_rows, HD), jnp.bfloat16),
            pltpu.VMEM((halo + tok_rows, HD), jnp.bfloat16),
            pltpu.SMEM((spans,), jnp.int32),
            pltpu.SMEM((HALO + span,), jnp.int32),
            pltpu.SMEM((VCAP,), jnp.int32),
        ],
        input_output_aliases=aliases,
        cost_estimate=pl.CostEstimate(
            flops=flops, bytes_accessed=4 * tok_rows * wide * heads, transcendentals=flops // 512
        ),
        compiler_params=pltpu.CompilerParams(vmem_limit_bytes=40 * 2**20),
        name="attend",
    )(*operands)


def local(spans, queries, keys, values, vertical, vert_count, slash, slash_count):
    tok_rows = queries.shape[0]
    heads = keys.shape[1] // HD
    span = tok_rows // BLK
    halo = HALO * BLK
    smem = pl.BlockSpec(memory_space=pltpu.SMEM)
    packed = pl.pallas_call(
        partial(pack_kernel, heads=heads, span=span),
        out_shape=[
            jax.ShapeDtypeStruct((TOGETHER, VCAP * BLK, 2 * HD), jnp.bfloat16)
            for _ in range(heads // TOGETHER)
        ],
        in_specs=[smem, smem, pl.BlockSpec(), pl.BlockSpec()],
        out_specs=[pl.BlockSpec() for _ in range(heads // TOGETHER)],
        name="pack",
    )(vertical, vert_count, keys, values)
    tail = jnp.concatenate([keys[tok_rows - halo :], values[tok_rows - halo :]], axis=1)
    left = lax.ppermute(tail, "ctx", [(i, i + 1) for i in range(spans - 1)])
    tables = (vertical, vert_count, slash, slash_count)
    out = None
    for i, part in enumerate(packed):
        everyone = lax.all_gather(part, "ctx", axis=0)
        out = attend(
            tables, queries, keys, values, left, everyone, out, i * TOGETHER, TOGETHER, spans
        )
    return out


def solution(mesh):
    placed = (
        P(("group", "ctx"), "head"),
        P(("group", "ctx"), "head"),
        P(("group", "ctx"), "head"),
        P(("group", "head"), None),
        P(("group", "head")),
        P(("group", "head"), None),
        P(("group", "head")),
    )
    return jax.shard_map(
        partial(local, mesh.shape["ctx"]),
        mesh=mesh, in_specs=placed, out_specs=P(("group", "ctx"), "head"), check_vma=False,
    )
```

```python
from functools import partial
import math

import jax
import jax.numpy as jnp
from jax import lax
from jax.experimental import pallas as pl
from jax.experimental.pallas import tpu as pltpu
from jax.sharding import PartitionSpec as P

HD = 128
BLK = 64
NV = 16
NS = 4
VCAP = 2
HALO = 5
CHUNK = 4
NEG = -1e30
UNROLL = 2
PARTS = 2


def pack_kernel(vert_ref, count_ref, keys_ref, vals_ref, packed, *, heads, span):
    lo = lax.axis_index("ctx") * span
    for h in range(heads):
        count = count_ref[h]
        first = jnp.int32(0)
        second = jnp.int32(0)
        seen = jnp.int32(0)
        for s in range(NV):
            at = vert_ref[h, s] - lo
            own = (s < count) & (at >= 0) & (at < span)
            first = jnp.where(own & (seen == 0), at, first)
            second = jnp.where(own & (seen == 1), at, second)
            seen = seen + own.astype(jnp.int32)
        lanes = slice(h * HD, (h + 1) * HD)
        for r, blk in enumerate((first, second)):
            rows = pl.ds(pl.multiple_of(blk * BLK, BLK), BLK)
            to = slice(r * BLK, (r + 1) * BLK)
            packed[h, to, :HD] = keys_ref[rows, lanes]
            packed[h, to, HD:] = vals_ref[rows, lanes]


def share_kernel(
    packed, keys_ref, vals_ref, all_ref, lk_ref, lv_ref,
    up_sem, over_sem, side_sem, halo_sem, recv_sem, halo_recv,
    *, heads, span, spans, cols,
):
    me = lax.axis_index("ctx")
    lo = me * span
    deep = spans // cols
    z, y = me // cols, me % cols
    has_up, has_down = z < deep - 1, z > 0
    is_last = y == cols - 1
    up, down, side = me + cols, me - cols, z * cols + (cols - 1 - y)
    per = heads // PARTS

    barrier = pltpu.get_barrier_semaphore()
    links = [(has_up, up), (has_down, down)]
    if cols > 1:
        links += [
            (z >= 0, side),
            (is_last & has_up, me + 1),
            ((y == 0) & has_down, me - 1),
        ]
    for there, peer in links:

        @pl.when(there)
        def _():
            pl.semaphore_signal(
                barrier, inc=1, device_id={"ctx": peer}, device_id_type=pl.DeviceIdType.MESH
            )

    pl.semaphore_wait(barrier, sum(there.astype(jnp.int32) for there, _ in links))

    def remote(src, dst, send, recv, peer):
        return pltpu.make_async_remote_copy(
            src_ref=src, dst_ref=dst, send_sem=send, recv_sem=recv,
            device_id={"ctx": peer}, device_id_type=pl.DeviceIdType.MESH,
        )

    def spot(src, part):
        return all_ref.at[src, pl.ds(part * per, per)]

    def chunk(src, part, send, peer, own):
        origin = packed.at[pl.ds(part * per, per)] if own else spot(src, part)
        return remote(origin, spot(src, part), send, recv_sem.at[src, part], peer)

    def arrived(src, part):
        chunk(src, part, up_sem.at[0, part], me, False).wait_recv()

    started = []

    def send(cond, copy):
        @pl.when(cond)
        def _():
            copy().start()

        started.append((cond, copy))

    def near_home(part):
        return cols > 1 and part < PARTS // 2

    tail = pl.ds(span * BLK - HALO * BLK, HALO * BLK)
    for k in range(deep):
        src = (z - k) * cols + y
        for part in range(PARTS):
            if k > 0:

                @pl.when(z >= k)
                def _():
                    arrived(src, part)

            if k < deep - 1:
                send(
                    has_up & (z >= k),
                    partial(chunk, src, part, up_sem.at[k, part], up, k == 0),
                )
            if cols > 1:
                cond = z >= k
                if k == 0:
                    cond = y == 0
                elif near_home(part):
                    cond = cond & is_last
                send(cond, partial(chunk, src, part, side_sem.at[k, part], side, k == 0))
        if k == 0:
            for i, (src_ref, dst_ref) in enumerate(((keys_ref, lk_ref), (vals_ref, lv_ref))):
                send(
                    me < spans - 1,
                    partial(
                        remote, src_ref.at[tail], dst_ref, halo_sem.at[i], halo_recv.at[i], me + 1
                    ),
                )
        if cols > 1:
            other = (z - k) * cols + (cols - 1 - y)
            for part in range(PARTS):
                if near_home(part):

                    @pl.when((z >= k) & is_last)
                    def _():
                        arrived(other, part)

                    if k < deep - 1:
                        send(
                            has_up & (z >= k) & is_last,
                            partial(chunk, other, part, over_sem.at[k, part], up, False),
                        )
    if cols > 1:
        for k in range(deep):
            other = (z - k) * cols + (cols - 1 - y)
            for part in range(PARTS):
                cond = (z >= k) & (y == 0) if near_home(part) else z >= k
                if k == 0:
                    cond = cond & is_last

                if not (k == 0 and near_home(part)):

                    @pl.when(cond)
                    def _():
                        arrived(other, part)

    @pl.when(me > 0)
    def _():
        for i, (src_ref, dst_ref) in enumerate(((keys_ref, lk_ref), (vals_ref, lv_ref))):
            remote(src_ref.at[tail], dst_ref, halo_sem.at[i], halo_recv.at[i], me).wait_recv()

    for cond, copy in started:

        @pl.when(cond)
        def _():
            copy().wait_send()


def attend_kernel(
    vert_ref, vcount_ref, slash_ref, scount_ref,
    q_ref, k_ref, v_ref, lk_ref, lv_ref, all_ref, *rest,
    span, group, spans, first_head,
):
    out_ref, kbuf, vbuf, kext, vext, used, near, own = rest[-8:]
    h = pl.program_id(0) + first_head
    lo = lax.axis_index("ctx") * span
    coef = math.log2(math.e) / math.sqrt(HD)

    @pl.when(pl.program_id(0) == 0)
    def _():
        kbuf[...] = jnp.zeros_like(kbuf)
        vbuf[:, :, :HD] = jnp.zeros(vbuf.shape[:2] + (HD,), jnp.bfloat16)
        vbuf[:, :, HD:] = jnp.ones(vbuf.shape[:2] + (HD,), jnp.bfloat16)

    halo = HALO * BLK
    kext[:halo, :] = lk_ref[...]
    vext[:halo, :] = lv_ref[...]
    kext[halo:, :] = k_ref[...]
    vext[halo:, :] = v_ref[...]
    for i in range(spans):
        used[i] = 0
    for i in range(HALO + span):
        near[i] = 0

    def take(u, n, at):
        to = pl.ds(pl.multiple_of(n * BLK, BLK), BLK)
        rows = pl.ds(pl.multiple_of(at * BLK, BLK), BLK)
        kbuf[u, to, :] = kext[rows, :]
        vbuf[u, to, :HD] = vext[rows, :]

    count = vcount_ref[h]

    def entry(s, state):
        n, mine = state
        blk = vert_ref[h, s]
        owner = blk // span
        rank = used[owner]
        used[owner] = rank + 1
        clean = blk < lo
        in_own = (blk >= lo) & (blk < lo + span)

        @pl.when(clean)
        def _():
            to = pl.ds(pl.multiple_of(n * BLK, BLK), BLK)
            rows = pl.ds(pl.multiple_of(rank * BLK, BLK), BLK)
            k_blk = all_ref[owner, 0, rows, :HD]
            v_blk = all_ref[owner, 0, rows, HD:]
            for u in range(UNROLL):
                kbuf[u, to, :] = k_blk
                vbuf[u, to, :HD] = v_blk

        @pl.when(in_own)
        def _():
            own[mine] = blk - lo

        at = blk - lo + HALO

        @pl.when((at >= 0) & (at < HALO + span))
        def _():
            near[at] = 1

        return n + clean.astype(jnp.int32), mine + in_own.astype(jnp.int32)

    shared, mine = lax.fori_loop(0, count, entry, (jnp.int32(1), jnp.int32(0)))
    slashes = scount_ref[h]
    tall = group * BLK
    pair = 2 * BLK

    def scores(u, chunks, l, n):
        width = chunks * CHUNK * BLK
        rows = pl.ds(pl.multiple_of(l * BLK, BLK), BLK)
        q = jnp.concatenate(
            [q_ref[rows, g * HD : (g + 1) * HD] for g in range(group)], axis=0
        )
        s = lax.dot_general(
            q, kbuf[u, :width, :], (((1,), (1,)), ((), ())), preferred_element_type=jnp.float32
        )
        row = lax.broadcasted_iota(jnp.int32, (tall, pair), 0) % BLK
        col = lax.broadcasted_iota(jnp.int32, (tall, pair), 1)
        parts = []
        for c in range(0, width, pair):
            part = s[:, c : c + pair]
            if c >= width - 2 * CHUNK * BLK:
                part = jnp.where(col < n * BLK - c, part, NEG)
            if c == 0:
                part = jnp.where((col <= row) | (col >= BLK), part, NEG)
            parts.append(part)
        return parts

    def body(chunks, ls, ns):
        width = chunks * CHUNK * BLK
        all_parts = [scores(u, chunks, l, n) for u, (l, n) in enumerate(zip(ls, ns))]
        probs = []
        for parts in all_parts:
            top = parts[0]
            for part in parts[1:]:
                top = jnp.maximum(top, part)
            top = jnp.max(top, axis=1, keepdims=True)
            probs.append(
                jnp.concatenate(
                    [jnp.exp2((part - top) * coef).astype(jnp.bfloat16) for part in parts], axis=1
                )
            )
        for u, (l, p) in enumerate(zip(ls, probs)):
            rows = pl.ds(pl.multiple_of(l * BLK, BLK), BLK)
            o = jnp.dot(p, vbuf[u, :width, :], preferred_element_type=jnp.float32)
            o = (o[:, :HD] / o[:, HD:]).astype(jnp.bfloat16)
            for g in range(group):
                out_ref[rows, g * HD : (g + 1) * HD] = o[g * BLK : (g + 1) * BLK, :]

    def fill(u, l):
        take(u, 0, l + HALO)
        n = shared
        for i in range(VCAP):
            use = (i < mine) & (own[i] < l)

            @pl.when(use)
            def _():
                take(u, n, own[i] + HALO)

            n = n + use.astype(jnp.int32)
        for j in range(1, NS):
            at = l + HALO - slash_ref[h, j]
            use = (j < slashes) & (at + lo >= HALO)
            use = use & (near[at] == 0)

            @pl.when(use)
            def _():
                take(u, n, at)

            n = n + use.astype(jnp.int32)
        return n

    def row_blocks(i, carry):
        ls = [i * UNROLL + u for u in range(UNROLL)]
        ns = [fill(u, l) for u, l in enumerate(ls)]
        most = ns[0]
        for n in ns[1:]:
            most = jnp.maximum(most, n)
        chunks = (most + CHUNK - 1) // CHUNK
        for c in range(1, (NV + NS) // CHUNK + 1):

            @pl.when(chunks == c)
            def _():
                body(c, ls, ns)

        return carry

    lax.fori_loop(0, span // UNROLL, row_blocks, 0)


def attend(tables, queries, keys, values, left_keys, left_vals, everyone, out, first_head, heads, spans):
    tok_rows, all_cols = queries.shape
    kv_heads = keys.shape[1] // HD
    wide = all_cols // kv_heads
    span = tok_rows // BLK
    halo = HALO * BLK
    cap = (NV + NS) * BLK
    smem = pl.BlockSpec(memory_space=pltpu.SMEM)
    operands = [*tables, queries, keys, values, left_keys, left_vals, everyone]
    in_specs = [
        smem, smem, smem, smem,
        pl.BlockSpec((tok_rows, wide), lambda h: (0, h + first_head)),
        pl.BlockSpec((tok_rows, HD), lambda h: (0, h + first_head)),
        pl.BlockSpec((tok_rows, HD), lambda h: (0, h + first_head)),
        pl.BlockSpec((halo, HD), lambda h: (0, h + first_head)),
        pl.BlockSpec((halo, HD), lambda h: (0, h + first_head)),
        pl.BlockSpec((spans, 1, VCAP * BLK, 2 * HD), lambda h: (0, h, 0, 0)),
    ]
    aliases = {}
    if out is not None:
        aliases = {len(operands): 0}
        operands.append(out)
        in_specs.append(pl.BlockSpec(memory_space=pl.ANY))
    flops = 2 * 2 * tok_rows * wide * cap * heads
    return pl.pallas_call(
        partial(
            attend_kernel, span=span, group=wide // HD, spans=spans, first_head=first_head
        ),
        grid=(heads,),
        out_shape=jax.ShapeDtypeStruct(queries.shape, jnp.bfloat16),
        in_specs=in_specs,
        out_specs=pl.BlockSpec((tok_rows, wide), lambda h: (0, h + first_head)),
        scratch_shapes=[
            pltpu.VMEM((UNROLL, cap, HD), jnp.bfloat16),
            pltpu.VMEM((UNROLL, cap, 2 * HD), jnp.bfloat16),
            pltpu.VMEM((halo + tok_rows, HD), jnp.bfloat16),
            pltpu.VMEM((halo + tok_rows, HD), jnp.bfloat16),
            pltpu.SMEM((spans,), jnp.int32),
            pltpu.SMEM((HALO + span,), jnp.int32),
            pltpu.SMEM((VCAP,), jnp.int32),
        ],
        input_output_aliases=aliases,
        cost_estimate=pl.CostEstimate(
            flops=flops, bytes_accessed=4 * tok_rows * wide * heads, transcendentals=flops // 512
        ),
        compiler_params=pltpu.CompilerParams(vmem_limit_bytes=40 * 2**20),
        name="attend",
    )(*operands)


def local(spans, queries, keys, values, vertical, vert_count, slash, slash_count):
    tok_rows, kv_cols = keys.shape
    heads = kv_cols // HD
    span = tok_rows // BLK
    cols = 2 if spans == 8 else 1
    deep = spans // cols
    smem = pl.BlockSpec(memory_space=pltpu.SMEM)
    vmem = pl.BlockSpec(memory_space=pltpu.VMEM)
    any_space = pl.BlockSpec(memory_space=pl.ANY)
    halo = jax.ShapeDtypeStruct((HALO * BLK, kv_cols), jnp.bfloat16)
    packed = pl.pallas_call(
        partial(pack_kernel, heads=heads, span=span),
        out_shape=jax.ShapeDtypeStruct((heads, VCAP * BLK, 2 * HD), jnp.bfloat16),
        in_specs=[smem, smem, vmem, vmem],
        out_specs=vmem,
        name="pack",
    )(vertical, vert_count, keys, values)
    everyone, left_keys, left_vals = pl.pallas_call(
        partial(share_kernel, heads=heads, span=span, spans=spans, cols=cols),
        out_shape=[
            jax.ShapeDtypeStruct((spans, heads, VCAP * BLK, 2 * HD), jnp.bfloat16), halo, halo
        ],
        in_specs=[vmem, any_space, any_space],
        out_specs=[any_space] * 3,
        scratch_shapes=[
            pltpu.SemaphoreType.DMA((deep, PARTS)),
            pltpu.SemaphoreType.DMA((deep, PARTS)),
            pltpu.SemaphoreType.DMA((deep, PARTS)),
            pltpu.SemaphoreType.DMA((2,)),
            pltpu.SemaphoreType.DMA((spans, PARTS)),
            pltpu.SemaphoreType.DMA((2,)),
        ],
        compiler_params=pltpu.CompilerParams(collective_id=0, has_side_effects=True),
        name="share",
    )(packed, keys, values)
    tables = (vertical, vert_count, slash, slash_count)
    return attend(
        tables, queries, keys, values, left_keys, left_vals, everyone, None, 0, heads, spans
    )


def solution(mesh):
    placed = (
        P(("group", "ctx"), "head"),
        P(("group", "ctx"), "head"),
        P(("group", "ctx"), "head"),
        P(("group", "head"), None),
        P(("group", "head")),
        P(("group", "head"), None),
        P(("group", "head")),
    )
    return jax.shard_map(
        partial(local, mesh.shape["ctx"]),
        mesh=mesh, in_specs=placed, out_specs=P(("group", "ctx"), "head"), check_vma=False,
    )
```

```python
from functools import partial
import math

import jax
import jax.numpy as jnp
from jax import lax
from jax.experimental import pallas as pl
from jax.experimental.pallas import tpu as pltpu
from jax.sharding import PartitionSpec as P

HD = 128
BLK = 64
NV = 16
NS = 4
VCAP = 2
HALO = 5
CHUNK = 4
NEG = -1e30
UNROLL = 3
PARTS = 2


def pack_kernel(vert_ref, count_ref, keys_ref, vals_ref, packed, *, heads, span):
    lo = lax.axis_index("ctx") * span
    for h in range(heads):
        count = count_ref[h]
        first = jnp.int32(0)
        second = jnp.int32(0)
        seen = jnp.int32(0)
        for s in range(NV):
            at = vert_ref[h, s] - lo
            own = (s < count) & (at >= 0) & (at < span)
            first = jnp.where(own & (seen == 0), at, first)
            second = jnp.where(own & (seen == 1), at, second)
            seen = seen + own.astype(jnp.int32)
        lanes = slice(h * HD, (h + 1) * HD)
        for r, blk in enumerate((first, second)):
            rows = pl.ds(pl.multiple_of(blk * BLK, BLK), BLK)
            to = slice(r * BLK, (r + 1) * BLK)
            packed[h, to, :HD] = keys_ref[rows, lanes]
            packed[h, to, HD:] = vals_ref[rows, lanes]


def share_kernel(
    packed, keys_ref, vals_ref, all_ref, lk_ref, lv_ref, relay_ref,
    up_sem, over_sem, side_sem, halo_sem, recv_sem, halo_recv, relay_sem, relay_recv, pass_sem,
    *, heads, span, spans, cols,
):
    me = lax.axis_index("ctx")
    lo = me * span
    deep = spans // cols
    z, y = me // cols, me % cols
    has_up, has_down = z < deep - 1, z > 0
    is_last = y == cols - 1
    up, down, side = me + cols, me - cols, z * cols + (cols - 1 - y)
    per = heads // PARTS

    barrier = pltpu.get_barrier_semaphore()
    links = [(has_up, up), (has_down, down)]
    if cols > 1:
        links.append((z >= 0, side))
    for there, peer in links:

        @pl.when(there)
        def _():
            pl.semaphore_signal(
                barrier, inc=1, device_id={"ctx": peer}, device_id_type=pl.DeviceIdType.MESH
            )

    pl.semaphore_wait(barrier, sum(there.astype(jnp.int32) for there, _ in links))

    def remote(src, dst, send, recv, peer):
        return pltpu.make_async_remote_copy(
            src_ref=src, dst_ref=dst, send_sem=send, recv_sem=recv,
            device_id={"ctx": peer}, device_id_type=pl.DeviceIdType.MESH,
        )

    def spot(src, part):
        return all_ref.at[src, pl.ds(part * per, per)]

    def chunk(src, part, send, peer, own):
        origin = packed.at[pl.ds(part * per, per)] if own else spot(src, part)
        return remote(origin, spot(src, part), send, recv_sem.at[src, part], peer)

    def arrived(src, part):
        chunk(src, part, up_sem.at[0, part], me, False).wait_recv()

    started = []

    def send(cond, copy):
        @pl.when(cond)
        def _():
            copy().start()

        started.append((cond, copy))

    def near_home(part):
        return cols > 1 and part < PARTS // 2

    tail = pl.ds(span * BLK - HALO * BLK, HALO * BLK)
    halos = ((keys_ref, lk_ref), (vals_ref, lv_ref))
    for k in range(deep):
        src = (z - k) * cols + y
        for part in range(PARTS):
            if k > 0:

                @pl.when(z >= k)
                def _():
                    arrived(src, part)

            if k < deep - 1:
                send(
                    has_up & (z >= k),
                    partial(chunk, src, part, up_sem.at[k, part], up, k == 0),
                )
            if cols > 1:
                cond = z >= k
                if k == 0:
                    cond = y == 0
                elif near_home(part):
                    cond = cond & is_last
                send(cond, partial(chunk, src, part, side_sem.at[k, part], side, k == 0))
        if k == 0:
            for i, (src_ref, dst_ref) in enumerate(halos):
                onward = is_last & has_up if cols > 1 else has_up
                if cols > 1:
                    send(
                        y == 0,
                        partial(
                            remote, src_ref.at[tail], dst_ref, halo_sem.at[i], halo_recv.at[i], side
                        ),
                    )
                send(
                    onward,
                    partial(
                        remote, src_ref.at[tail], relay_ref.at[i], relay_sem.at[i],
                        relay_recv.at[i], side,
                    )
                    if cols > 1
                    else partial(
                        remote, src_ref.at[tail], dst_ref, halo_sem.at[i], halo_recv.at[i], up
                    ),
                )
        elif cols > 1 and k <= 2:
            i = k - 1
            relay = partial(
                remote, relay_ref.at[i], halos[i][1], pass_sem.at[i], halo_recv.at[i], up
            )

            @pl.when((y == 0) & has_up)
            def _():
                remote(
                    relay_ref.at[i], relay_ref.at[i], relay_sem.at[i], relay_recv.at[i], side
                ).wait_recv()

            send((y == 0) & has_up, relay)
        if cols > 1:
            other = (z - k) * cols + (cols - 1 - y)
            for part in range(PARTS):
                if near_home(part):

                    @pl.when((z >= k) & is_last)
                    def _():
                        arrived(other, part)

                    if k < deep - 1:
                        send(
                            has_up & (z >= k) & is_last,
                            partial(chunk, other, part, over_sem.at[k, part], up, False),
                        )
    if cols > 1:
        for k in range(deep):
            other = (z - k) * cols + (cols - 1 - y)
            for part in range(PARTS):
                cond = (z >= k) & (y == 0) if near_home(part) else z >= k
                if k == 0:
                    cond = cond & is_last

                if not (k == 0 and near_home(part)):

                    @pl.when(cond)
                    def _():
                        arrived(other, part)

    @pl.when(me > 0)
    def _():
        for i, (src_ref, dst_ref) in enumerate(halos):
            remote(src_ref.at[tail], dst_ref, halo_sem.at[i], halo_recv.at[i], me).wait_recv()

    for cond, copy in started:

        @pl.when(cond)
        def _():
            copy().wait_send()


def attend_kernel(
    vert_ref, vcount_ref, slash_ref, scount_ref,
    q_ref, k_ref, v_ref, lk_ref, lv_ref, all_ref, *rest,
    span, group, spans, first_head,
):
    out_ref, kbuf, vbuf, kext, vext, used, near, own = rest[-8:]
    h = pl.program_id(0) + first_head
    lo = lax.axis_index("ctx") * span
    coef = math.log2(math.e) / math.sqrt(HD)

    @pl.when(pl.program_id(0) == 0)
    def _():
        kbuf[...] = jnp.zeros_like(kbuf)
        vbuf[:, :, :HD] = jnp.zeros(vbuf.shape[:2] + (HD,), jnp.bfloat16)
        vbuf[:, :, HD:] = jnp.ones(vbuf.shape[:2] + (HD,), jnp.bfloat16)

    halo = HALO * BLK
    kext[:halo, :] = lk_ref[...]
    vext[:halo, :] = lv_ref[...]
    kext[halo:, :] = k_ref[...]
    vext[halo:, :] = v_ref[...]
    for i in range(spans):
        used[i] = 0
    for i in range(HALO + span):
        near[i] = 0

    def take(u, n, at):
        to = pl.ds(pl.multiple_of(n * BLK, BLK), BLK)
        rows = pl.ds(pl.multiple_of(at * BLK, BLK), BLK)
        kbuf[u, to, :] = kext[rows, :]
        vbuf[u, to, :HD] = vext[rows, :]

    count = vcount_ref[h]

    def entry(s, state):
        n, mine = state
        blk = vert_ref[h, s]
        owner = blk // span
        rank = used[owner]
        used[owner] = rank + 1
        clean = blk < lo
        in_own = (blk >= lo) & (blk < lo + span)

        @pl.when(clean)
        def _():
            to = pl.ds(pl.multiple_of(n * BLK, BLK), BLK)
            rows = pl.ds(pl.multiple_of(rank * BLK, BLK), BLK)
            k_blk = all_ref[owner, 0, rows, :HD]
            v_blk = all_ref[owner, 0, rows, HD:]
            for u in range(UNROLL):
                kbuf[u, to, :] = k_blk
                vbuf[u, to, :HD] = v_blk

        @pl.when(in_own)
        def _():
            own[mine] = blk - lo

        at = blk - lo + HALO

        @pl.when((at >= 0) & (at < HALO + span))
        def _():
            near[at] = 1

        return n + clean.astype(jnp.int32), mine + in_own.astype(jnp.int32)

    shared, mine = lax.fori_loop(0, count, entry, (jnp.int32(1), jnp.int32(0)))
    slashes = scount_ref[h]
    tall = group * BLK
    pair = 2 * BLK

    def scores(u, chunks, l, n):
        width = chunks * CHUNK * BLK
        rows = pl.ds(pl.multiple_of(l * BLK, BLK), BLK)
        q = jnp.concatenate(
            [q_ref[rows, g * HD : (g + 1) * HD] for g in range(group)], axis=0
        )
        s = lax.dot_general(
            q, kbuf[u, :width, :], (((1,), (1,)), ((), ())), preferred_element_type=jnp.float32
        )
        row = lax.broadcasted_iota(jnp.int32, (tall, pair), 0) % BLK
        col = lax.broadcasted_iota(jnp.int32, (tall, pair), 1)
        parts = []
        for c in range(0, width, pair):
            part = s[:, c : c + pair]
            if c >= width - 2 * CHUNK * BLK:
                part = jnp.where(col < n * BLK - c, part, NEG)
            if c == 0:
                part = jnp.where((col <= row) | (col >= BLK), part, NEG)
            parts.append(part)
        return parts

    def body(chunks, ls, ns):
        width = chunks * CHUNK * BLK
        all_parts = [scores(u, chunks, l, n) for u, (l, n) in enumerate(zip(ls, ns))]
        probs = []
        for parts in all_parts:
            top = parts[0]
            for part in parts[1:]:
                top = jnp.maximum(top, part)
            top = jnp.max(top, axis=1, keepdims=True)
            probs.append(
                jnp.concatenate(
                    [jnp.exp2((part - top) * coef).astype(jnp.bfloat16) for part in parts], axis=1
                )
            )
        for u, (l, p) in enumerate(zip(ls, probs)):
            rows = pl.ds(pl.multiple_of(l * BLK, BLK), BLK)
            o = jnp.dot(p, vbuf[u, :width, :], preferred_element_type=jnp.float32)
            o = (o[:, :HD] / o[:, HD:]).astype(jnp.bfloat16)
            for g in range(group):
                out_ref[rows, g * HD : (g + 1) * HD] = o[g * BLK : (g + 1) * BLK, :]

    def fill(u, l):
        take(u, 0, l + HALO)
        n = shared
        for i in range(VCAP):
            use = (i < mine) & (own[i] < l)

            @pl.when(use)
            def _():
                take(u, n, own[i] + HALO)

            n = n + use.astype(jnp.int32)
        for j in range(1, NS):
            at = l + HALO - slash_ref[h, j]
            use = (j < slashes) & (at + lo >= HALO)
            use = use & (near[at] == 0)

            @pl.when(use)
            def _():
                take(u, n, at)

            n = n + use.astype(jnp.int32)
        return n

    def row_blocks(i, carry):
        ls = [i * UNROLL + u for u in range(UNROLL)]
        ns = [fill(u, l) for u, l in enumerate(ls)]
        most = ns[0]
        for n in ns[1:]:
            most = jnp.maximum(most, n)
        chunks = (most + CHUNK - 1) // CHUNK
        for c in range(1, (NV + NS) // CHUNK + 1):

            @pl.when(chunks == c)
            def _():
                body(c, ls, ns)

        return carry

    lax.fori_loop(0, span // UNROLL, row_blocks, 0)


def attend(tables, queries, keys, values, left_keys, left_vals, everyone, out, first_head, heads, spans):
    tok_rows, all_cols = queries.shape
    kv_heads = keys.shape[1] // HD
    wide = all_cols // kv_heads
    span = tok_rows // BLK
    halo = HALO * BLK
    cap = (NV + NS) * BLK
    smem = pl.BlockSpec(memory_space=pltpu.SMEM)
    operands = [*tables, queries, keys, values, left_keys, left_vals, everyone]
    in_specs = [
        smem, smem, smem, smem,
        pl.BlockSpec((tok_rows, wide), lambda h: (0, h + first_head)),
        pl.BlockSpec((tok_rows, HD), lambda h: (0, h + first_head)),
        pl.BlockSpec((tok_rows, HD), lambda h: (0, h + first_head)),
        pl.BlockSpec((halo, HD), lambda h: (0, h + first_head)),
        pl.BlockSpec((halo, HD), lambda h: (0, h + first_head)),
        pl.BlockSpec((spans, 1, VCAP * BLK, 2 * HD), lambda h: (0, h, 0, 0)),
    ]
    aliases = {}
    if out is not None:
        aliases = {len(operands): 0}
        operands.append(out)
        in_specs.append(pl.BlockSpec(memory_space=pl.ANY))
    flops = 2 * 2 * tok_rows * wide * cap * heads
    return pl.pallas_call(
        partial(
            attend_kernel, span=span, group=wide // HD, spans=spans, first_head=first_head
        ),
        grid=(heads,),
        out_shape=jax.ShapeDtypeStruct(queries.shape, jnp.bfloat16),
        in_specs=in_specs,
        out_specs=pl.BlockSpec((tok_rows, wide), lambda h: (0, h + first_head)),
        scratch_shapes=[
            pltpu.VMEM((UNROLL, cap, HD), jnp.bfloat16),
            pltpu.VMEM((UNROLL, cap, 2 * HD), jnp.bfloat16),
            pltpu.VMEM((halo + tok_rows, HD), jnp.bfloat16),
            pltpu.VMEM((halo + tok_rows, HD), jnp.bfloat16),
            pltpu.SMEM((spans,), jnp.int32),
            pltpu.SMEM((HALO + span,), jnp.int32),
            pltpu.SMEM((VCAP,), jnp.int32),
        ],
        input_output_aliases=aliases,
        cost_estimate=pl.CostEstimate(
            flops=flops, bytes_accessed=4 * tok_rows * wide * heads, transcendentals=flops // 512
        ),
        compiler_params=pltpu.CompilerParams(vmem_limit_bytes=60 * 2**20),
        name="attend",
    )(*operands)


def local(spans, queries, keys, values, vertical, vert_count, slash, slash_count):
    tok_rows, kv_cols = keys.shape
    heads = kv_cols // HD
    span = tok_rows // BLK
    cols = 2 if spans == 8 else 1
    deep = spans // cols
    smem = pl.BlockSpec(memory_space=pltpu.SMEM)
    vmem = pl.BlockSpec(memory_space=pltpu.VMEM)
    any_space = pl.BlockSpec(memory_space=pl.ANY)
    halo = jax.ShapeDtypeStruct((HALO * BLK, kv_cols), jnp.bfloat16)
    packed = pl.pallas_call(
        partial(pack_kernel, heads=heads, span=span),
        out_shape=jax.ShapeDtypeStruct((heads, VCAP * BLK, 2 * HD), jnp.bfloat16),
        in_specs=[smem, smem, vmem, vmem],
        out_specs=vmem,
        name="pack",
    )(vertical, vert_count, keys, values)
    everyone, left_keys, left_vals, _ = pl.pallas_call(
        partial(share_kernel, heads=heads, span=span, spans=spans, cols=cols),
        out_shape=[
            jax.ShapeDtypeStruct((spans, heads, VCAP * BLK, 2 * HD), jnp.bfloat16),
            halo,
            halo,
            jax.ShapeDtypeStruct((2, HALO * BLK, kv_cols), jnp.bfloat16),
        ],
        in_specs=[vmem, any_space, any_space],
        out_specs=[any_space] * 4,
        scratch_shapes=[
            pltpu.SemaphoreType.DMA((deep, PARTS)),
            pltpu.SemaphoreType.DMA((deep, PARTS)),
            pltpu.SemaphoreType.DMA((deep, PARTS)),
            pltpu.SemaphoreType.DMA((2,)),
            pltpu.SemaphoreType.DMA((spans, PARTS)),
            pltpu.SemaphoreType.DMA((2,)),
            pltpu.SemaphoreType.DMA((2,)),
            pltpu.SemaphoreType.DMA((2,)),
            pltpu.SemaphoreType.DMA((2,)),
        ],
        compiler_params=pltpu.CompilerParams(collective_id=0, has_side_effects=True),
        name="share",
    )(packed, keys, values)
    tables = (vertical, vert_count, slash, slash_count)
    return attend(
        tables, queries, keys, values, left_keys, left_vals, everyone, None, 0, heads, spans
    )


def solution(mesh):
    placed = (
        P(("group", "ctx"), "head"),
        P(("group", "ctx"), "head"),
        P(("group", "ctx"), "head"),
        P(("group", "head"), None),
        P(("group", "head")),
        P(("group", "head"), None),
        P(("group", "head")),
    )
    return jax.shard_map(
        partial(local, mesh.shape["ctx"]),
        mesh=mesh, in_specs=placed, out_specs=P(("group", "ctx"), "head"), check_vma=False,
    )
```

```python
from functools import partial
import math

import jax
import jax.numpy as jnp
from jax import lax
from jax.experimental import pallas as pl
from jax.experimental.pallas import tpu as pltpu
from jax.sharding import PartitionSpec as P

HD = 128
BLK = 64
NV = 16
NS = 4
VCAP = 2
HALO = 5
CHUNK = 4
NEG = -1e30
UNROLL = 3
PARTS = 2
EXTRA = 3


def pack_kernel(vert_ref, count_ref, keys_ref, vals_ref, packed, *, heads, span):
    lo = lax.axis_index("ctx") * span
    for h in range(heads):
        count = count_ref[h]
        first = jnp.int32(0)
        second = jnp.int32(0)
        seen = jnp.int32(0)
        for s in range(NV):
            at = vert_ref[h, s] - lo
            own = (s < count) & (at >= 0) & (at < span)
            first = jnp.where(own & (seen == 0), at, first)
            second = jnp.where(own & (seen == 1), at, second)
            seen = seen + own.astype(jnp.int32)
        lanes = slice(h * HD, (h + 1) * HD)
        for r, blk in enumerate((first, second)):
            rows = pl.ds(pl.multiple_of(blk * BLK, BLK), BLK)
            to = slice(r * BLK, (r + 1) * BLK)
            packed[h, to, :HD] = keys_ref[rows, lanes]
            packed[h, to, HD:] = vals_ref[rows, lanes]


def share_kernel(
    packed, keys_ref, vals_ref, all_ref, lk_ref, lv_ref, relay_ref,
    up_sem, over_sem, side_sem, halo_sem, recv_sem, halo_recv, relay_sem, relay_recv, pass_sem,
    *, heads, span, spans, cols,
):
    me = lax.axis_index("ctx")
    lo = me * span
    deep = spans // cols
    z, y = me // cols, me % cols
    has_up, has_down = z < deep - 1, z > 0
    is_last = y == cols - 1
    up, down, side = me + cols, me - cols, z * cols + (cols - 1 - y)
    per = heads // PARTS

    barrier = pltpu.get_barrier_semaphore()
    links = [(has_up, up), (has_down, down)]
    if cols > 1:
        links.append((z >= 0, side))
    for there, peer in links:

        @pl.when(there)
        def _():
            pl.semaphore_signal(
                barrier, inc=1, device_id={"ctx": peer}, device_id_type=pl.DeviceIdType.MESH
            )

    pl.semaphore_wait(barrier, sum(there.astype(jnp.int32) for there, _ in links))

    def remote(src, dst, send, recv, peer):
        return pltpu.make_async_remote_copy(
            src_ref=src, dst_ref=dst, send_sem=send, recv_sem=recv,
            device_id={"ctx": peer}, device_id_type=pl.DeviceIdType.MESH,
        )

    def spot(src, part):
        return all_ref.at[src, pl.ds(part * per, per)]

    def chunk(src, part, send, peer, own):
        origin = packed.at[pl.ds(part * per, per)] if own else spot(src, part)
        return remote(origin, spot(src, part), send, recv_sem.at[src, part], peer)

    def arrived(src, part):
        chunk(src, part, up_sem.at[0, part], me, False).wait_recv()

    started = []

    def send(cond, copy):
        @pl.when(cond)
        def _():
            copy().start()

        started.append((cond, copy))

    def near_home(part):
        return cols > 1 and part < PARTS // 2

    tail = pl.ds(span * BLK - HALO * BLK, HALO * BLK)
    halos = ((keys_ref, lk_ref), (vals_ref, lv_ref))
    for k in range(deep):
        src = (z - k) * cols + y
        for part in range(PARTS):
            if k > 0:

                @pl.when(z >= k)
                def _():
                    arrived(src, part)

            if k < deep - 1:
                send(
                    has_up & (z >= k),
                    partial(chunk, src, part, up_sem.at[k, part], up, k == 0),
                )
            if cols > 1:
                cond = z >= k
                if k == 0:
                    cond = y == 0
                elif near_home(part):
                    cond = cond & is_last
                send(cond, partial(chunk, src, part, side_sem.at[k, part], side, k == 0))
        if k == 0:
            for i, (src_ref, dst_ref) in enumerate(halos):
                onward = is_last & has_up if cols > 1 else has_up
                if cols > 1:
                    send(
                        y == 0,
                        partial(
                            remote, src_ref.at[tail], dst_ref, halo_sem.at[i], halo_recv.at[i], side
                        ),
                    )
                send(
                    onward,
                    partial(
                        remote, src_ref.at[tail], relay_ref.at[i], relay_sem.at[i],
                        relay_recv.at[i], side,
                    )
                    if cols > 1
                    else partial(
                        remote, src_ref.at[tail], dst_ref, halo_sem.at[i], halo_recv.at[i], up
                    ),
                )
        elif cols > 1 and k <= 2:
            i = k - 1
            relay = partial(
                remote, relay_ref.at[i], halos[i][1], pass_sem.at[i], halo_recv.at[i], up
            )

            @pl.when((y == 0) & has_up)
            def _():
                remote(
                    relay_ref.at[i], relay_ref.at[i], relay_sem.at[i], relay_recv.at[i], side
                ).wait_recv()

            send((y == 0) & has_up, relay)
        if cols > 1:
            other = (z - k) * cols + (cols - 1 - y)
            for part in range(PARTS):
                if near_home(part):

                    @pl.when((z >= k) & is_last)
                    def _():
                        arrived(other, part)

                    if k < deep - 1:
                        send(
                            has_up & (z >= k) & is_last,
                            partial(chunk, other, part, over_sem.at[k, part], up, False),
                        )
    if cols > 1:
        for k in range(deep):
            other = (z - k) * cols + (cols - 1 - y)
            for part in range(PARTS):
                cond = (z >= k) & (y == 0) if near_home(part) else z >= k
                if k == 0:
                    cond = cond & is_last

                if not (k == 0 and near_home(part)):

                    @pl.when(cond)
                    def _():
                        arrived(other, part)

    @pl.when(me > 0)
    def _():
        for i, (src_ref, dst_ref) in enumerate(halos):
            remote(src_ref.at[tail], dst_ref, halo_sem.at[i], halo_recv.at[i], me).wait_recv()

    for cond, copy in started:

        @pl.when(cond)
        def _():
            copy().wait_send()


def attend_kernel(
    vert_ref, vcount_ref, slash_ref, scount_ref,
    q_ref, k_ref, v_ref, lk_ref, lv_ref, all_ref, *rest,
    span, group, spans, first_head,
):
    out_ref, kall, vall, kbuf, vbuf, kext, vext, used, near, own = rest[-10:]
    h = pl.program_id(0) + first_head
    lo = lax.axis_index("ctx") * span
    coef = math.log2(math.e) / math.sqrt(HD)

    @pl.when(pl.program_id(0) == 0)
    def _():
        kbuf[...] = jnp.zeros_like(kbuf)
        vbuf[:, :, :HD] = jnp.zeros(vbuf.shape[:2] + (HD,), jnp.bfloat16)
        vbuf[:, :, HD:] = jnp.ones(vbuf.shape[:2] + (HD,), jnp.bfloat16)
        vall[:, HD:] = jnp.ones((vall.shape[0], HD), jnp.bfloat16)

    halo = HALO * BLK
    kext[:halo, :] = lk_ref[...]
    vext[:halo, :] = lv_ref[...]
    kext[halo:, :] = k_ref[...]
    vext[halo:, :] = v_ref[...]
    for i in range(spans):
        used[i] = 0
    for i in range(HALO + span):
        near[i] = 0

    def take(u, n, at):
        to = pl.ds(pl.multiple_of(n * BLK, BLK), BLK)
        rows = pl.ds(pl.multiple_of(at * BLK, BLK), BLK)
        kbuf[u, to, :] = kext[rows, :]
        vbuf[u, to, :HD] = vext[rows, :]

    count = vcount_ref[h]

    def entry(s, state):
        n, mine = state
        blk = vert_ref[h, s]
        owner = blk // span
        rank = used[owner]
        used[owner] = rank + 1
        clean = blk < lo
        in_own = (blk >= lo) & (blk < lo + span)

        @pl.when(clean)
        def _():
            to = pl.ds(pl.multiple_of(n * BLK, BLK), BLK)
            rows = pl.ds(pl.multiple_of(rank * BLK, BLK), BLK)
            kall[to, :] = all_ref[owner, 0, rows, :HD]
            vall[to, :HD] = all_ref[owner, 0, rows, HD:]

        @pl.when(in_own)
        def _():
            own[mine] = blk - lo

        at = blk - lo + HALO

        @pl.when((at >= 0) & (at < HALO + span))
        def _():
            near[at] = 1

        return n + clean.astype(jnp.int32), mine + in_own.astype(jnp.int32)

    found, mine = lax.fori_loop(0, count, entry, (jnp.int32(0), jnp.int32(0)))
    whole = found // CHUNK
    over = found - whole * CHUNK
    for i in range(CHUNK - 1):

        @pl.when(i < over)
        def _():
            rows = pl.ds(pl.multiple_of((whole * CHUNK + i) * BLK, BLK), BLK)
            to = slice((1 + i) * BLK, (2 + i) * BLK)
            for u in range(UNROLL):
                kbuf[u, to, :] = kall[rows, :]
                vbuf[u, to, :HD] = vall[rows, :HD]

    shared = over + 1
    slashes = scount_ref[h]
    tall = group * BLK
    pair = 2 * BLK

    def score(q, k):
        return lax.dot_general(
            q, k, (((1,), (1,)), ((), ())), preferred_element_type=jnp.float32
        )

    def masked(s, n):
        width = s.shape[1]
        row = lax.broadcasted_iota(jnp.int32, (tall, pair), 0) % BLK
        col = lax.broadcasted_iota(jnp.int32, (tall, pair), 1)
        parts = []
        for c in range(0, width, pair):
            part = s[:, c : c + pair]
            if c >= width - 2 * CHUNK * BLK:
                part = jnp.where(col < n * BLK - c, part, NEG)
            if c == 0:
                part = jnp.where((col <= row) | (col >= BLK), part, NEG)
            parts.append(part)
        return parts

    def body(full, chunks, ls, ns):
        common = full * CHUNK * BLK
        width = chunks * CHUNK * BLK
        rows = [pl.ds(pl.multiple_of(l * BLK, BLK), BLK) for l in ls]
        qs = [
            jnp.concatenate([q_ref[r, g * HD : (g + 1) * HD] for g in range(group)], axis=0)
            for r in rows
        ]
        if full:
            s_all = score(jnp.concatenate(qs, axis=0), kall[:common, :])
        common_probs, probs = [], []
        for u, (q, n) in enumerate(zip(qs, ns)):
            parts = masked(score(q, kbuf[u, :width, :]), n)
            extra = len(parts)
            if full:
                mine_all = s_all[u * tall : (u + 1) * tall]
                parts += [mine_all[:, c : c + pair] for c in range(0, common, pair)]
            top = parts[0]
            for part in parts[1:]:
                top = jnp.maximum(top, part)
            top = jnp.max(top, axis=1, keepdims=True)
            weights = [jnp.exp2((part - top) * coef).astype(jnp.bfloat16) for part in parts]
            probs.append(jnp.concatenate(weights[:extra], axis=1))
            if full:
                common_probs.append(jnp.concatenate(weights[extra:], axis=1))
        if full:
            o_all = jnp.dot(
                jnp.concatenate(common_probs, axis=0), vall[:common, :],
                preferred_element_type=jnp.float32,
            )
        for u, (r, p) in enumerate(zip(rows, probs)):
            o = jnp.dot(p, vbuf[u, :width, :], preferred_element_type=jnp.float32)
            if full:
                o = o + o_all[u * tall : (u + 1) * tall]
            o = (o[:, :HD] / o[:, HD:]).astype(jnp.bfloat16)
            for g in range(group):
                out_ref[r, g * HD : (g + 1) * HD] = o[g * BLK : (g + 1) * BLK, :]

    def fill(u, l):
        take(u, 0, l + HALO)
        n = shared
        for i in range(VCAP):
            use = (i < mine) & (own[i] < l)

            @pl.when(use)
            def _():
                take(u, n, own[i] + HALO)

            n = n + use.astype(jnp.int32)
        for j in range(1, NS):
            at = l + HALO - slash_ref[h, j]
            use = (j < slashes) & (at + lo >= HALO)
            use = use & (near[at] == 0)

            @pl.when(use)
            def _():
                take(u, n, at)

            n = n + use.astype(jnp.int32)
        return n

    def row_blocks(i, carry):
        ls = [i * UNROLL + u for u in range(UNROLL)]
        ns = [fill(u, l) for u, l in enumerate(ls)]
        most = ns[0]
        for n in ns[1:]:
            most = jnp.maximum(most, n)
        chunks = (most + CHUNK - 1) // CHUNK
        for full in range(NV // CHUNK + 1):
            for c in range(1, EXTRA + 1):

                @pl.when((whole == full) & (chunks == c))
                def _():
                    body(full, c, ls, ns)

        return carry

    lax.fori_loop(0, span // UNROLL, row_blocks, 0)


def attend(tables, queries, keys, values, left_keys, left_vals, everyone, out, first_head, heads, spans):
    tok_rows, all_cols = queries.shape
    kv_heads = keys.shape[1] // HD
    wide = all_cols // kv_heads
    span = tok_rows // BLK
    halo = HALO * BLK
    cap = (NV + NS) * BLK
    smem = pl.BlockSpec(memory_space=pltpu.SMEM)
    operands = [*tables, queries, keys, values, left_keys, left_vals, everyone]
    in_specs = [
        smem, smem, smem, smem,
        pl.BlockSpec((tok_rows, wide), lambda h: (0, h + first_head)),
        pl.BlockSpec((tok_rows, HD), lambda h: (0, h + first_head)),
        pl.BlockSpec((tok_rows, HD), lambda h: (0, h + first_head)),
        pl.BlockSpec((halo, HD), lambda h: (0, h + first_head)),
        pl.BlockSpec((halo, HD), lambda h: (0, h + first_head)),
        pl.BlockSpec((spans, 1, VCAP * BLK, 2 * HD), lambda h: (0, h, 0, 0)),
    ]
    aliases = {}
    if out is not None:
        aliases = {len(operands): 0}
        operands.append(out)
        in_specs.append(pl.BlockSpec(memory_space=pl.ANY))
    flops = 2 * 2 * tok_rows * wide * cap * heads
    return pl.pallas_call(
        partial(
            attend_kernel, span=span, group=wide // HD, spans=spans, first_head=first_head
        ),
        grid=(heads,),
        out_shape=jax.ShapeDtypeStruct(queries.shape, jnp.bfloat16),
        in_specs=in_specs,
        out_specs=pl.BlockSpec((tok_rows, wide), lambda h: (0, h + first_head)),
        scratch_shapes=[
            pltpu.VMEM((NV * BLK, HD), jnp.bfloat16),
            pltpu.VMEM((NV * BLK, 2 * HD), jnp.bfloat16),
            pltpu.VMEM((UNROLL, EXTRA * CHUNK * BLK, HD), jnp.bfloat16),
            pltpu.VMEM((UNROLL, EXTRA * CHUNK * BLK, 2 * HD), jnp.bfloat16),
            pltpu.VMEM((halo + tok_rows, HD), jnp.bfloat16),
            pltpu.VMEM((halo + tok_rows, HD), jnp.bfloat16),
            pltpu.SMEM((spans,), jnp.int32),
            pltpu.SMEM((HALO + span,), jnp.int32),
            pltpu.SMEM((VCAP,), jnp.int32),
        ],
        input_output_aliases=aliases,
        cost_estimate=pl.CostEstimate(
            flops=flops, bytes_accessed=4 * tok_rows * wide * heads, transcendentals=flops // 512
        ),
        compiler_params=pltpu.CompilerParams(vmem_limit_bytes=60 * 2**20),
        name="attend",
    )(*operands)


def local(spans, queries, keys, values, vertical, vert_count, slash, slash_count):
    tok_rows, kv_cols = keys.shape
    heads = kv_cols // HD
    span = tok_rows // BLK
    cols = 2 if spans == 8 else 1
    deep = spans // cols
    smem = pl.BlockSpec(memory_space=pltpu.SMEM)
    vmem = pl.BlockSpec(memory_space=pltpu.VMEM)
    any_space = pl.BlockSpec(memory_space=pl.ANY)
    halo = jax.ShapeDtypeStruct((HALO * BLK, kv_cols), jnp.bfloat16)
    packed = pl.pallas_call(
        partial(pack_kernel, heads=heads, span=span),
        out_shape=jax.ShapeDtypeStruct((heads, VCAP * BLK, 2 * HD), jnp.bfloat16),
        in_specs=[smem, smem, vmem, vmem],
        out_specs=vmem,
        name="pack",
    )(vertical, vert_count, keys, values)
    everyone, left_keys, left_vals, _ = pl.pallas_call(
        partial(share_kernel, heads=heads, span=span, spans=spans, cols=cols),
        out_shape=[
            jax.ShapeDtypeStruct((spans, heads, VCAP * BLK, 2 * HD), jnp.bfloat16),
            halo,
            halo,
            jax.ShapeDtypeStruct((2, HALO * BLK, kv_cols), jnp.bfloat16),
        ],
        in_specs=[vmem, any_space, any_space],
        out_specs=[any_space] * 4,
        scratch_shapes=[
            pltpu.SemaphoreType.DMA((deep, PARTS)),
            pltpu.SemaphoreType.DMA((deep, PARTS)),
            pltpu.SemaphoreType.DMA((deep, PARTS)),
            pltpu.SemaphoreType.DMA((2,)),
            pltpu.SemaphoreType.DMA((spans, PARTS)),
            pltpu.SemaphoreType.DMA((2,)),
            pltpu.SemaphoreType.DMA((2,)),
            pltpu.SemaphoreType.DMA((2,)),
            pltpu.SemaphoreType.DMA((2,)),
        ],
        compiler_params=pltpu.CompilerParams(collective_id=0, has_side_effects=True),
        name="share",
    )(packed, keys, values)
    tables = (vertical, vert_count, slash, slash_count)
    return attend(
        tables, queries, keys, values, left_keys, left_vals, everyone, None, 0, heads, spans
    )


def solution(mesh):
    placed = (
        P(("group", "ctx"), "head"),
        P(("group", "ctx"), "head"),
        P(("group", "ctx"), "head"),
        P(("group", "head"), None),
        P(("group", "head")),
        P(("group", "head"), None),
        P(("group", "head")),
    )
    return jax.shard_map(
        partial(local, mesh.shape["ctx"]),
        mesh=mesh, in_specs=placed, out_specs=P(("group", "ctx"), "head"), check_vma=False,
    )
```

```python
from functools import partial
import math

import jax
import jax.numpy as jnp
from jax import lax
from jax.experimental import pallas as pl
from jax.experimental.pallas import tpu as pltpu
from jax.sharding import PartitionSpec as P

HD = 128
BLK = 64
NV = 16
NS = 4
VCAP = 2
HALO = 5
CHUNK = 2
NEG = -1e30
UNROLL = 3
PARTS = 2


def pack_kernel(vert_ref, count_ref, keys_ref, vals_ref, packed, *, heads, span):
    lo = lax.axis_index("ctx") * span
    for h in range(heads):
        count = count_ref[h]
        first = jnp.int32(0)
        second = jnp.int32(0)
        seen = jnp.int32(0)
        for s in range(NV):
            at = vert_ref[h, s] - lo
            own = (s < count) & (at >= 0) & (at < span)
            first = jnp.where(own & (seen == 0), at, first)
            second = jnp.where(own & (seen == 1), at, second)
            seen = seen + own.astype(jnp.int32)
        lanes = slice(h * HD, (h + 1) * HD)
        for r, blk in enumerate((first, second)):
            rows = pl.ds(pl.multiple_of(blk * BLK, BLK), BLK)
            to = slice(r * BLK, (r + 1) * BLK)
            packed[h, to, :HD] = keys_ref[rows, lanes]
            packed[h, to, HD:] = vals_ref[rows, lanes]


def share_kernel(
    packed, keys_ref, vals_ref, all_ref, lk_ref, lv_ref, relay_ref,
    up_sem, over_sem, side_sem, halo_sem, recv_sem, halo_recv, relay_sem, relay_recv, pass_sem,
    *, heads, span, spans, cols,
):
    me = lax.axis_index("ctx")
    lo = me * span
    deep = spans // cols
    z, y = me // cols, me % cols
    has_up, has_down = z < deep - 1, z > 0
    is_last = y == cols - 1
    up, down, side = me + cols, me - cols, z * cols + (cols - 1 - y)
    per = heads // PARTS

    barrier = pltpu.get_barrier_semaphore()
    links = [(has_up, up), (has_down, down)]
    if cols > 1:
        links.append((z >= 0, side))
    for there, peer in links:

        @pl.when(there)
        def _():
            pl.semaphore_signal(
                barrier, inc=1, device_id={"ctx": peer}, device_id_type=pl.DeviceIdType.MESH
            )

    pl.semaphore_wait(barrier, sum(there.astype(jnp.int32) for there, _ in links))

    def remote(src, dst, send, recv, peer):
        return pltpu.make_async_remote_copy(
            src_ref=src, dst_ref=dst, send_sem=send, recv_sem=recv,
            device_id={"ctx": peer}, device_id_type=pl.DeviceIdType.MESH,
        )

    def spot(src, part):
        return all_ref.at[src, pl.ds(part * per, per)]

    def chunk(src, part, send, peer, own):
        origin = packed.at[pl.ds(part * per, per)] if own else spot(src, part)
        return remote(origin, spot(src, part), send, recv_sem.at[src, part], peer)

    def arrived(src, part):
        chunk(src, part, up_sem.at[0, part], me, False).wait_recv()

    started = []

    def send(cond, copy):
        @pl.when(cond)
        def _():
            copy().start()

        started.append((cond, copy))

    def near_home(part):
        return cols > 1 and part < PARTS // 2

    tail = pl.ds(span * BLK - HALO * BLK, HALO * BLK)
    halos = ((keys_ref, lk_ref), (vals_ref, lv_ref))
    for k in range(deep):
        src = (z - k) * cols + y
        for part in range(PARTS):
            if k > 0:

                @pl.when(z >= k)
                def _():
                    arrived(src, part)

            if k < deep - 1:
                send(
                    has_up & (z >= k),
                    partial(chunk, src, part, up_sem.at[k, part], up, k == 0),
                )
            if cols > 1:
                cond = z >= k
                if k == 0:
                    cond = y == 0
                elif near_home(part):
                    cond = cond & is_last
                send(cond, partial(chunk, src, part, side_sem.at[k, part], side, k == 0))
        if k == 0:
            for i, (src_ref, dst_ref) in enumerate(halos):
                onward = is_last & has_up if cols > 1 else has_up
                if cols > 1:
                    send(
                        y == 0,
                        partial(
                            remote, src_ref.at[tail], dst_ref, halo_sem.at[i], halo_recv.at[i], side
                        ),
                    )
                send(
                    onward,
                    partial(
                        remote, src_ref.at[tail], relay_ref.at[i], relay_sem.at[i],
                        relay_recv.at[i], side,
                    )
                    if cols > 1
                    else partial(
                        remote, src_ref.at[tail], dst_ref, halo_sem.at[i], halo_recv.at[i], up
                    ),
                )
        elif cols > 1 and k <= 2:
            i = k - 1
            relay = partial(
                remote, relay_ref.at[i], halos[i][1], pass_sem.at[i], halo_recv.at[i], up
            )

            @pl.when((y == 0) & has_up)
            def _():
                remote(
                    relay_ref.at[i], relay_ref.at[i], relay_sem.at[i], relay_recv.at[i], side
                ).wait_recv()

            send((y == 0) & has_up, relay)
        if cols > 1:
            other = (z - k) * cols + (cols - 1 - y)
            for part in range(PARTS):
                if near_home(part):

                    @pl.when((z >= k) & is_last)
                    def _():
                        arrived(other, part)

                    if k < deep - 1:
                        send(
                            has_up & (z >= k) & is_last,
                            partial(chunk, other, part, over_sem.at[k, part], up, False),
                        )
    if cols > 1:
        for k in range(deep):
            other = (z - k) * cols + (cols - 1 - y)
            for part in range(PARTS):
                cond = (z >= k) & (y == 0) if near_home(part) else z >= k
                if k == 0:
                    cond = cond & is_last

                if not (k == 0 and near_home(part)):

                    @pl.when(cond)
                    def _():
                        arrived(other, part)

    @pl.when(me > 0)
    def _():
        for i, (src_ref, dst_ref) in enumerate(halos):
            remote(src_ref.at[tail], dst_ref, halo_sem.at[i], halo_recv.at[i], me).wait_recv()

    for cond, copy in started:

        @pl.when(cond)
        def _():
            copy().wait_send()


def attend_kernel(
    vert_ref, vcount_ref, slash_ref, scount_ref,
    q_ref, k_ref, v_ref, lk_ref, lv_ref, all_ref, *rest,
    span, group, spans, first_head,
):
    out_ref, kbuf, vbuf, kext, vext, used, near, own = rest[-8:]
    h = pl.program_id(0) + first_head
    lo = lax.axis_index("ctx") * span
    coef = math.log2(math.e) / math.sqrt(HD)

    @pl.when(pl.program_id(0) == 0)
    def _():
        kbuf[...] = jnp.zeros_like(kbuf)
        vbuf[:, :, :HD] = jnp.zeros(vbuf.shape[:2] + (HD,), jnp.bfloat16)
        vbuf[:, :, HD:] = jnp.ones(vbuf.shape[:2] + (HD,), jnp.bfloat16)

    halo = HALO * BLK
    kext[:halo, :] = lk_ref[...]
    vext[:halo, :] = lv_ref[...]
    kext[halo:, :] = k_ref[...]
    vext[halo:, :] = v_ref[...]
    for i in range(spans):
        used[i] = 0
    for i in range(HALO + span):
        near[i] = 0

    def take(u, n, at):
        to = pl.ds(pl.multiple_of(n * BLK, BLK), BLK)
        rows = pl.ds(pl.multiple_of(at * BLK, BLK), BLK)
        kbuf[u, to, :] = kext[rows, :]
        vbuf[u, to, :HD] = vext[rows, :]

    count = vcount_ref[h]

    def entry(s, state):
        n, mine = state
        blk = vert_ref[h, s]
        owner = blk // span
        rank = used[owner]
        used[owner] = rank + 1
        clean = blk < lo
        in_own = (blk >= lo) & (blk < lo + span)

        @pl.when(clean)
        def _():
            to = pl.ds(pl.multiple_of(n * BLK, BLK), BLK)
            rows = pl.ds(pl.multiple_of(rank * BLK, BLK), BLK)
            k_blk = all_ref[owner, 0, rows, :HD]
            v_blk = all_ref[owner, 0, rows, HD:]
            for u in range(UNROLL):
                kbuf[u, to, :] = k_blk
                vbuf[u, to, :HD] = v_blk

        @pl.when(in_own)
        def _():
            own[mine] = blk - lo

        at = blk - lo + HALO

        @pl.when((at >= 0) & (at < HALO + span))
        def _():
            near[at] = 1

        return n + clean.astype(jnp.int32), mine + in_own.astype(jnp.int32)

    shared, mine = lax.fori_loop(0, count, entry, (jnp.int32(1), jnp.int32(0)))
    slashes = scount_ref[h]
    tall = group * BLK
    pair = 2 * BLK

    def scores(u, chunks, l, n):
        width = chunks * CHUNK * BLK
        rows = pl.ds(pl.multiple_of(l * BLK, BLK), BLK)
        q = jnp.concatenate(
            [q_ref[rows, g * HD : (g + 1) * HD] for g in range(group)], axis=0
        )
        s = lax.dot_general(
            q, kbuf[u, :width, :], (((1,), (1,)), ((), ())), preferred_element_type=jnp.float32
        )
        row = lax.broadcasted_iota(jnp.int32, (tall, pair), 0) % BLK
        col = lax.broadcasted_iota(jnp.int32, (tall, pair), 1)
        parts = []
        for c in range(0, width, pair):
            part = s[:, c : c + pair]
            if c + pair > width - (CHUNK - 1 + VCAP + NS - 1) * BLK:
                part = jnp.where(col < n * BLK - c, part, NEG)
            if c == 0:
                part = jnp.where((col <= row) | (col >= BLK), part, NEG)
            parts.append(part)
        return parts

    def body(chunks, ls, ns):
        width = chunks * CHUNK * BLK
        all_parts = [scores(u, chunks, l, n) for u, (l, n) in enumerate(zip(ls, ns))]
        probs = []
        for parts in all_parts:
            top = parts[0]
            for part in parts[1:]:
                top = jnp.maximum(top, part)
            top = jnp.max(top, axis=1, keepdims=True)
            probs.append(
                jnp.concatenate(
                    [jnp.exp2((part - top) * coef).astype(jnp.bfloat16) for part in parts], axis=1
                )
            )
        for u, (l, p) in enumerate(zip(ls, probs)):
            rows = pl.ds(pl.multiple_of(l * BLK, BLK), BLK)
            o = jnp.dot(p, vbuf[u, :width, :], preferred_element_type=jnp.float32)
            o = (o[:, :HD] / o[:, HD:]).astype(jnp.bfloat16)
            for g in range(group):
                out_ref[rows, g * HD : (g + 1) * HD] = o[g * BLK : (g + 1) * BLK, :]

    def fill(u, l):
        take(u, 0, l + HALO)
        n = shared
        for i in range(VCAP):
            use = (i < mine) & (own[i] < l)

            @pl.when(use)
            def _():
                take(u, n, own[i] + HALO)

            n = n + use.astype(jnp.int32)
        for j in range(1, NS):
            at = l + HALO - slash_ref[h, j]
            use = (j < slashes) & (at + lo >= HALO)
            use = use & (near[at] == 0)

            @pl.when(use)
            def _():
                take(u, n, at)

            n = n + use.astype(jnp.int32)
        return n

    def row_blocks(i, carry):
        ls = [i * UNROLL + u for u in range(UNROLL)]
        ns = [fill(u, l) for u, l in enumerate(ls)]
        most = ns[0]
        for n in ns[1:]:
            most = jnp.maximum(most, n)
        chunks = (most + CHUNK - 1) // CHUNK
        for c in range(1, (NV + NS) // CHUNK + 1):

            @pl.when(chunks == c)
            def _():
                body(c, ls, ns)

        return carry

    lax.fori_loop(0, span // UNROLL, row_blocks, 0)


def attend(tables, queries, keys, values, left_keys, left_vals, everyone, out, first_head, heads, spans):
    tok_rows, all_cols = queries.shape
    kv_heads = keys.shape[1] // HD
    wide = all_cols // kv_heads
    span = tok_rows // BLK
    halo = HALO * BLK
    cap = (NV + NS) * BLK
    smem = pl.BlockSpec(memory_space=pltpu.SMEM)
    operands = [*tables, queries, keys, values, left_keys, left_vals, everyone]
    in_specs = [
        smem, smem, smem, smem,
        pl.BlockSpec((tok_rows, wide), lambda h: (0, h + first_head)),
        pl.BlockSpec((tok_rows, HD), lambda h: (0, h + first_head)),
        pl.BlockSpec((tok_rows, HD), lambda h: (0, h + first_head)),
        pl.BlockSpec((halo, HD), lambda h: (0, h + first_head)),
        pl.BlockSpec((halo, HD), lambda h: (0, h + first_head)),
        pl.BlockSpec((spans, 1, VCAP * BLK, 2 * HD), lambda h: (0, h, 0, 0)),
    ]
    aliases = {}
    if out is not None:
        aliases = {len(operands): 0}
        operands.append(out)
        in_specs.append(pl.BlockSpec(memory_space=pl.ANY))
    flops = 2 * 2 * tok_rows * wide * cap * heads
    return pl.pallas_call(
        partial(
            attend_kernel, span=span, group=wide // HD, spans=spans, first_head=first_head
        ),
        grid=(heads,),
        out_shape=jax.ShapeDtypeStruct(queries.shape, jnp.bfloat16),
        in_specs=in_specs,
        out_specs=pl.BlockSpec((tok_rows, wide), lambda h: (0, h + first_head)),
        scratch_shapes=[
            pltpu.VMEM((UNROLL, cap, HD), jnp.bfloat16),
            pltpu.VMEM((UNROLL, cap, 2 * HD), jnp.bfloat16),
            pltpu.VMEM((halo + tok_rows, HD), jnp.bfloat16),
            pltpu.VMEM((halo + tok_rows, HD), jnp.bfloat16),
            pltpu.SMEM((spans,), jnp.int32),
            pltpu.SMEM((HALO + span,), jnp.int32),
            pltpu.SMEM((VCAP,), jnp.int32),
        ],
        input_output_aliases=aliases,
        cost_estimate=pl.CostEstimate(
            flops=flops, bytes_accessed=4 * tok_rows * wide * heads, transcendentals=flops // 512
        ),
        compiler_params=pltpu.CompilerParams(vmem_limit_bytes=60 * 2**20),
        name="attend",
    )(*operands)


def local(spans, queries, keys, values, vertical, vert_count, slash, slash_count):
    tok_rows, kv_cols = keys.shape
    heads = kv_cols // HD
    span = tok_rows // BLK
    cols = 2 if spans == 8 else 1
    deep = spans // cols
    smem = pl.BlockSpec(memory_space=pltpu.SMEM)
    vmem = pl.BlockSpec(memory_space=pltpu.VMEM)
    any_space = pl.BlockSpec(memory_space=pl.ANY)
    halo = jax.ShapeDtypeStruct((HALO * BLK, kv_cols), jnp.bfloat16)
    packed = pl.pallas_call(
        partial(pack_kernel, heads=heads, span=span),
        out_shape=jax.ShapeDtypeStruct((heads, VCAP * BLK, 2 * HD), jnp.bfloat16),
        in_specs=[smem, smem, vmem, vmem],
        out_specs=vmem,
        name="pack",
    )(vertical, vert_count, keys, values)
    everyone, left_keys, left_vals, _ = pl.pallas_call(
        partial(share_kernel, heads=heads, span=span, spans=spans, cols=cols),
        out_shape=[
            jax.ShapeDtypeStruct((spans, heads, VCAP * BLK, 2 * HD), jnp.bfloat16),
            halo,
            halo,
            jax.ShapeDtypeStruct((2, HALO * BLK, kv_cols), jnp.bfloat16),
        ],
        in_specs=[vmem, any_space, any_space],
        out_specs=[any_space] * 4,
        scratch_shapes=[
            pltpu.SemaphoreType.DMA((deep, PARTS)),
            pltpu.SemaphoreType.DMA((deep, PARTS)),
            pltpu.SemaphoreType.DMA((deep, PARTS)),
            pltpu.SemaphoreType.DMA((2,)),
            pltpu.SemaphoreType.DMA((spans, PARTS)),
            pltpu.SemaphoreType.DMA((2,)),
            pltpu.SemaphoreType.DMA((2,)),
            pltpu.SemaphoreType.DMA((2,)),
            pltpu.SemaphoreType.DMA((2,)),
        ],
        compiler_params=pltpu.CompilerParams(collective_id=0, has_side_effects=True),
        name="share",
    )(packed, keys, values)
    tables = (vertical, vert_count, slash, slash_count)
    return attend(
        tables, queries, keys, values, left_keys, left_vals, everyone, None, 0, heads, spans
    )


def solution(mesh):
    placed = (
        P(("group", "ctx"), "head"),
        P(("group", "ctx"), "head"),
        P(("group", "ctx"), "head"),
        P(("group", "head"), None),
        P(("group", "head")),
        P(("group", "head"), None),
        P(("group", "head")),
    )
    return jax.shard_map(
        partial(local, mesh.shape["ctx"]),
        mesh=mesh, in_specs=placed, out_specs=P(("group", "ctx"), "head"), check_vma=False,
    )
```

```python
from functools import partial
import math

import jax
import jax.numpy as jnp
from jax import lax
from jax.experimental import pallas as pl
from jax.experimental.pallas import tpu as pltpu
from jax.sharding import PartitionSpec as P

HD = 128
BLK = 64
NV = 16
NS = 4
VCAP = 2
HALO = 5
CHUNK = 4
NEG = -1e30
UNROLL = 4
PARTS = 2


def pack_kernel(vert_ref, count_ref, keys_ref, vals_ref, packed, *, heads, span):
    lo = lax.axis_index("ctx") * span
    for h in range(heads):
        count = count_ref[h]
        first = jnp.int32(0)
        second = jnp.int32(0)
        seen = jnp.int32(0)
        for s in range(NV):
            at = vert_ref[h, s] - lo
            own = (s < count) & (at >= 0) & (at < span)
            first = jnp.where(own & (seen == 0), at, first)
            second = jnp.where(own & (seen == 1), at, second)
            seen = seen + own.astype(jnp.int32)
        lanes = slice(h * HD, (h + 1) * HD)
        for r, blk in enumerate((first, second)):
            rows = pl.ds(pl.multiple_of(blk * BLK, BLK), BLK)
            to = slice(r * BLK, (r + 1) * BLK)
            packed[h, to, :HD] = keys_ref[rows, lanes]
            packed[h, to, HD:] = vals_ref[rows, lanes]


def share_kernel(
    packed, keys_ref, vals_ref, all_ref, lk_ref, lv_ref, relay_ref,
    up_sem, over_sem, side_sem, halo_sem, recv_sem, halo_recv, relay_sem, relay_recv, pass_sem,
    *, heads, span, spans, cols,
):
    me = lax.axis_index("ctx")
    lo = me * span
    deep = spans // cols
    z, y = me // cols, me % cols
    has_up, has_down = z < deep - 1, z > 0
    is_last = y == cols - 1
    up, down, side = me + cols, me - cols, z * cols + (cols - 1 - y)
    per = heads // PARTS

    barrier = pltpu.get_barrier_semaphore()
    links = [(has_up, up), (has_down, down)]
    if cols > 1:
        links.append((z >= 0, side))
    for there, peer in links:

        @pl.when(there)
        def _():
            pl.semaphore_signal(
                barrier, inc=1, device_id={"ctx": peer}, device_id_type=pl.DeviceIdType.MESH
            )

    pl.semaphore_wait(barrier, sum(there.astype(jnp.int32) for there, _ in links))

    def remote(src, dst, send, recv, peer):
        return pltpu.make_async_remote_copy(
            src_ref=src, dst_ref=dst, send_sem=send, recv_sem=recv,
            device_id={"ctx": peer}, device_id_type=pl.DeviceIdType.MESH,
        )

    def spot(src, part):
        return all_ref.at[src, pl.ds(part * per, per)]

    def chunk(src, part, send, peer, own):
        origin = packed.at[pl.ds(part * per, per)] if own else spot(src, part)
        return remote(origin, spot(src, part), send, recv_sem.at[src, part], peer)

    def arrived(src, part):
        chunk(src, part, up_sem.at[0, part], me, False).wait_recv()

    started = []

    def send(cond, copy):
        @pl.when(cond)
        def _():
            copy().start()

        started.append((cond, copy))

    def near_home(part):
        return cols > 1 and part < PARTS // 2

    tail = pl.ds(span * BLK - HALO * BLK, HALO * BLK)
    halos = ((keys_ref, lk_ref), (vals_ref, lv_ref))
    for k in range(deep):
        src = (z - k) * cols + y
        for part in range(PARTS):
            if k > 0:

                @pl.when(z >= k)
                def _():
                    arrived(src, part)

            if k < deep - 1:
                send(
                    has_up & (z >= k),
                    partial(chunk, src, part, up_sem.at[k, part], up, k == 0),
                )
            if cols > 1:
                cond = z >= k
                if k == 0:
                    cond = y == 0
                elif near_home(part):
                    cond = cond & is_last
                send(cond, partial(chunk, src, part, side_sem.at[k, part], side, k == 0))
        if k == 0:
            for i, (src_ref, dst_ref) in enumerate(halos):
                onward = is_last & has_up if cols > 1 else has_up
                if cols > 1:
                    send(
                        y == 0,
                        partial(
                            remote, src_ref.at[tail], dst_ref, halo_sem.at[i], halo_recv.at[i], side
                        ),
                    )
                send(
                    onward,
                    partial(
                        remote, src_ref.at[tail], relay_ref.at[i], relay_sem.at[i],
                        relay_recv.at[i], side,
                    )
                    if cols > 1
                    else partial(
                        remote, src_ref.at[tail], dst_ref, halo_sem.at[i], halo_recv.at[i], up
                    ),
                )
        elif cols > 1 and k <= 2:
            i = k - 1
            relay = partial(
                remote, relay_ref.at[i], halos[i][1], pass_sem.at[i], halo_recv.at[i], up
            )

            @pl.when((y == 0) & has_up)
            def _():
                remote(
                    relay_ref.at[i], relay_ref.at[i], relay_sem.at[i], relay_recv.at[i], side
                ).wait_recv()

            send((y == 0) & has_up, relay)
        if cols > 1:
            other = (z - k) * cols + (cols - 1 - y)
            for part in range(PARTS):
                if near_home(part):

                    @pl.when((z >= k) & is_last)
                    def _():
                        arrived(other, part)

                    if k < deep - 1:
                        send(
                            has_up & (z >= k) & is_last,
                            partial(chunk, other, part, over_sem.at[k, part], up, False),
                        )
    if cols > 1:
        for k in range(deep):
            other = (z - k) * cols + (cols - 1 - y)
            for part in range(PARTS):
                cond = (z >= k) & (y == 0) if near_home(part) else z >= k
                if k == 0:
                    cond = cond & is_last

                if not (k == 0 and near_home(part)):

                    @pl.when(cond)
                    def _():
                        arrived(other, part)

    @pl.when(me > 0)
    def _():
        for i, (src_ref, dst_ref) in enumerate(halos):
            remote(src_ref.at[tail], dst_ref, halo_sem.at[i], halo_recv.at[i], me).wait_recv()

    for cond, copy in started:

        @pl.when(cond)
        def _():
            copy().wait_send()


def attend_kernel(
    vert_ref, vcount_ref, slash_ref, scount_ref,
    q_ref, k_ref, v_ref, lk_ref, lv_ref, all_ref, *rest,
    span, group, spans, first_head,
):
    out_ref, kbuf, vbuf, kext, vext, used, near, own = rest[-8:]
    h = pl.program_id(0) + first_head
    lo = lax.axis_index("ctx") * span
    coef = math.log2(math.e) / math.sqrt(HD)

    @pl.when(pl.program_id(0) == 0)
    def _():
        kbuf[...] = jnp.zeros_like(kbuf)
        vbuf[:, :, :HD] = jnp.zeros(vbuf.shape[:2] + (HD,), jnp.bfloat16)
        vbuf[:, :, HD:] = jnp.ones(vbuf.shape[:2] + (HD,), jnp.bfloat16)

    halo = HALO * BLK
    kext[:halo, :] = lk_ref[...]
    vext[:halo, :] = lv_ref[...]
    kext[halo:, :] = k_ref[...]
    vext[halo:, :] = v_ref[...]
    for i in range(spans):
        used[i] = 0
    for i in range(HALO + span):
        near[i] = 0

    def take(u, n, at):
        to = pl.ds(pl.multiple_of(n * BLK, BLK), BLK)
        rows = pl.ds(pl.multiple_of(at * BLK, BLK), BLK)
        kbuf[u, to, :] = kext[rows, :]
        vbuf[u, to, :HD] = vext[rows, :]

    count = vcount_ref[h]

    def entry(s, state):
        n, mine = state
        blk = vert_ref[h, s]
        owner = blk // span
        rank = used[owner]
        used[owner] = rank + 1
        clean = blk < lo
        in_own = (blk >= lo) & (blk < lo + span)

        @pl.when(clean)
        def _():
            to = pl.ds(pl.multiple_of(n * BLK, BLK), BLK)
            rows = pl.ds(pl.multiple_of(rank * BLK, BLK), BLK)
            k_blk = all_ref[owner, 0, rows, :HD]
            v_blk = all_ref[owner, 0, rows, HD:]
            for u in range(UNROLL):
                kbuf[u, to, :] = k_blk
                vbuf[u, to, :HD] = v_blk

        @pl.when(in_own)
        def _():
            own[mine] = blk - lo

        at = blk - lo + HALO

        @pl.when((at >= 0) & (at < HALO + span))
        def _():
            near[at] = 1

        return n + clean.astype(jnp.int32), mine + in_own.astype(jnp.int32)

    shared, mine = lax.fori_loop(0, count, entry, (jnp.int32(1), jnp.int32(0)))
    slashes = scount_ref[h]
    tall = group * BLK
    pair = 2 * BLK

    def scores(u, chunks, l, n):
        width = chunks * CHUNK * BLK
        rows = pl.ds(pl.multiple_of(l * BLK, BLK), BLK)
        q = jnp.concatenate(
            [q_ref[rows, g * HD : (g + 1) * HD] for g in range(group)], axis=0
        )
        s = lax.dot_general(
            q, kbuf[u, :width, :], (((1,), (1,)), ((), ())), preferred_element_type=jnp.float32
        )
        row = lax.broadcasted_iota(jnp.int32, (tall, pair), 0) % BLK
        col = lax.broadcasted_iota(jnp.int32, (tall, pair), 1)
        parts = []
        for c in range(0, width, pair):
            part = s[:, c : c + pair]
            if c >= width - 2 * CHUNK * BLK:
                part = jnp.where(col < n * BLK - c, part, NEG)
            if c == 0:
                part = jnp.where((col <= row) | (col >= BLK), part, NEG)
            parts.append(part)
        return parts

    def body(chunks, ls, ns):
        width = chunks * CHUNK * BLK
        all_parts = [scores(u, chunks, l, n) for u, (l, n) in enumerate(zip(ls, ns))]
        probs = []
        for parts in all_parts:
            top = parts[0]
            for part in parts[1:]:
                top = jnp.maximum(top, part)
            top = jnp.max(top, axis=1, keepdims=True)
            probs.append(
                jnp.concatenate(
                    [jnp.exp2((part - top) * coef).astype(jnp.bfloat16) for part in parts], axis=1
                )
            )
        for u, (l, p) in enumerate(zip(ls, probs)):
            rows = pl.ds(pl.multiple_of(l * BLK, BLK), BLK)
            o = jnp.dot(p, vbuf[u, :width, :], preferred_element_type=jnp.float32)
            o = (o[:, :HD] / o[:, HD:]).astype(jnp.bfloat16)
            for g in range(group):
                out_ref[rows, g * HD : (g + 1) * HD] = o[g * BLK : (g + 1) * BLK, :]

    def fill(u, l):
        take(u, 0, l + HALO)
        n = shared
        for i in range(VCAP):
            use = (i < mine) & (own[i] < l)

            @pl.when(use)
            def _():
                take(u, n, own[i] + HALO)

            n = n + use.astype(jnp.int32)
        for j in range(1, NS):
            at = l + HALO - slash_ref[h, j]
            use = (j < slashes) & (at + lo >= HALO)
            use = use & (near[at] == 0)

            @pl.when(use)
            def _():
                take(u, n, at)

            n = n + use.astype(jnp.int32)
        return n

    def row_blocks(i, carry):
        ls = [i * UNROLL + u for u in range(UNROLL)]
        ns = [fill(u, l) for u, l in enumerate(ls)]
        most = ns[0]
        for n in ns[1:]:
            most = jnp.maximum(most, n)
        chunks = (most + CHUNK - 1) // CHUNK
        for c in range(1, (NV + NS) // CHUNK + 1):

            @pl.when(chunks == c)
            def _():
                body(c, ls, ns)

        return carry

    lax.fori_loop(0, span // UNROLL, row_blocks, 0)


def attend(tables, queries, keys, values, left_keys, left_vals, everyone, out, first_head, heads, spans):
    tok_rows, all_cols = queries.shape
    kv_heads = keys.shape[1] // HD
    wide = all_cols // kv_heads
    span = tok_rows // BLK
    halo = HALO * BLK
    cap = (NV + NS) * BLK
    smem = pl.BlockSpec(memory_space=pltpu.SMEM)
    operands = [*tables, queries, keys, values, left_keys, left_vals, everyone]
    in_specs = [
        smem, smem, smem, smem,
        pl.BlockSpec((tok_rows, wide), lambda h: (0, h + first_head)),
        pl.BlockSpec((tok_rows, HD), lambda h: (0, h + first_head)),
        pl.BlockSpec((tok_rows, HD), lambda h: (0, h + first_head)),
        pl.BlockSpec((halo, HD), lambda h: (0, h + first_head)),
        pl.BlockSpec((halo, HD), lambda h: (0, h + first_head)),
        pl.BlockSpec((spans, 1, VCAP * BLK, 2 * HD), lambda h: (0, h, 0, 0)),
    ]
    aliases = {}
    if out is not None:
        aliases = {len(operands): 0}
        operands.append(out)
        in_specs.append(pl.BlockSpec(memory_space=pl.ANY))
    flops = 2 * 2 * tok_rows * wide * cap * heads
    return pl.pallas_call(
        partial(
            attend_kernel, span=span, group=wide // HD, spans=spans, first_head=first_head
        ),
        grid=(heads,),
        out_shape=jax.ShapeDtypeStruct(queries.shape, jnp.bfloat16),
        in_specs=in_specs,
        out_specs=pl.BlockSpec((tok_rows, wide), lambda h: (0, h + first_head)),
        scratch_shapes=[
            pltpu.VMEM((UNROLL, cap, HD), jnp.bfloat16),
            pltpu.VMEM((UNROLL, cap, 2 * HD), jnp.bfloat16),
            pltpu.VMEM((halo + tok_rows, HD), jnp.bfloat16),
            pltpu.VMEM((halo + tok_rows, HD), jnp.bfloat16),
            pltpu.SMEM((spans,), jnp.int32),
            pltpu.SMEM((HALO + span,), jnp.int32),
            pltpu.SMEM((VCAP,), jnp.int32),
        ],
        input_output_aliases=aliases,
        cost_estimate=pl.CostEstimate(
            flops=flops, bytes_accessed=4 * tok_rows * wide * heads, transcendentals=flops // 512
        ),
        compiler_params=pltpu.CompilerParams(vmem_limit_bytes=60 * 2**20),
        name="attend",
    )(*operands)


def local(spans, queries, keys, values, vertical, vert_count, slash, slash_count):
    tok_rows, kv_cols = keys.shape
    heads = kv_cols // HD
    span = tok_rows // BLK
    cols = 2 if spans == 8 else 1
    deep = spans // cols
    smem = pl.BlockSpec(memory_space=pltpu.SMEM)
    vmem = pl.BlockSpec(memory_space=pltpu.VMEM)
    any_space = pl.BlockSpec(memory_space=pl.ANY)
    halo = jax.ShapeDtypeStruct((HALO * BLK, kv_cols), jnp.bfloat16)
    packed = pl.pallas_call(
        partial(pack_kernel, heads=heads, span=span),
        out_shape=jax.ShapeDtypeStruct((heads, VCAP * BLK, 2 * HD), jnp.bfloat16),
        in_specs=[smem, smem, vmem, vmem],
        out_specs=vmem,
        name="pack",
    )(vertical, vert_count, keys, values)
    everyone, left_keys, left_vals, _ = pl.pallas_call(
        partial(share_kernel, heads=heads, span=span, spans=spans, cols=cols),
        out_shape=[
            jax.ShapeDtypeStruct((spans, heads, VCAP * BLK, 2 * HD), jnp.bfloat16),
            halo,
            halo,
            jax.ShapeDtypeStruct((2, HALO * BLK, kv_cols), jnp.bfloat16),
        ],
        in_specs=[vmem, any_space, any_space],
        out_specs=[any_space] * 4,
        scratch_shapes=[
            pltpu.SemaphoreType.DMA((deep, PARTS)),
            pltpu.SemaphoreType.DMA((deep, PARTS)),
            pltpu.SemaphoreType.DMA((deep, PARTS)),
            pltpu.SemaphoreType.DMA((2,)),
            pltpu.SemaphoreType.DMA((spans, PARTS)),
            pltpu.SemaphoreType.DMA((2,)),
            pltpu.SemaphoreType.DMA((2,)),
            pltpu.SemaphoreType.DMA((2,)),
            pltpu.SemaphoreType.DMA((2,)),
        ],
        compiler_params=pltpu.CompilerParams(collective_id=0, has_side_effects=True),
        name="share",
    )(packed, keys, values)
    tables = (vertical, vert_count, slash, slash_count)
    return attend(
        tables, queries, keys, values, left_keys, left_vals, everyone, None, 0, heads, spans
    )


def solution(mesh):
    placed = (
        P(("group", "ctx"), "head"),
        P(("group", "ctx"), "head"),
        P(("group", "ctx"), "head"),
        P(("group", "head"), None),
        P(("group", "head")),
        P(("group", "head"), None),
        P(("group", "head")),
    )
    return jax.shard_map(
        partial(local, mesh.shape["ctx"]),
        mesh=mesh, in_specs=placed, out_specs=P(("group", "ctx"), "head"), check_vma=False,
    )
```
